256 devices in a mesh: coh: 4 (over y), lat: 4 (over x), lon: 16 (over z, core).
Axes of the slice: x: 4, y: 4, z: 8, core: 2. Of those that a mesh axis runs over, the one named last changes fastest.
Arguments:
- saved_period_abundance: bfloat16 [2, 128, 256, 4096], P(None, 'coh', 'lat', 'lon'), may hold values from 0.099609375 to 2
- final_abundance_sensitivity: bfloat16 [128, 256, 4096], P('coh', 'lat', 'lon'), may hold values from -6 to 6
- prey_biomass: float32 [2, 256, 4096], P(None, 'lat', 'lon'), may hold values from 0.2 to 2
- water_heat_field: float32 [2, 256, 4096], P(None, 'lat', 'lon'), may hold values from 10 to 30
- marine_indicator: int32 [256, 4096], P('lat', 'lon'), may hold values 0 or 1
- fishing_pressure: float32 [256, 4096], P('lat', 'lon'), may hold values from 0.1 to 2
- offspring_yield: float32 [256, 4096], P('lat', 'lon'), may hold values from 2 to 20
- death_fraction: float32 [128], P('coh'), may hold values from 0.01 to 0.5
- gear_vulnerability: float32 [128], P('coh'), may hold values from 0.05 to 0.5
- spreading_coefficient: float32 [128], P('coh'), may hold values from 0.02 to 0.12
- directed_drift_rate: float32 [128], P('coh'), may hold values from 0.01 to 0.06
- favoured_thermal_level: float32 [128], P('coh'), may hold values from 12 to 28
- breeding_contribution: float32 [128], P('coh'), may hold values from 0.005 to 0.03
- landing_error_sensitivity: float32 [2048, 2, 128], P(('lat', 'lon'), None, 'coh'), may hold values from -6 to 6
- fleet_east_piece: int32 [2048, 1], P(('lat', 'lon')), may hold values from 0 to 15; in each aligned block of 32 rows (0 to 31, 32 to 63, ...) at most 3 rows name the same one
- fleet_north_piece: int32 [2048], P(('lat', 'lon')), may hold values from 0 to 3
- fleet_area_patch: int32 [2048], P(('lat', 'lon')), may hold values from 0 to 31
- fleet_age_bounds: int32 [2048, 2], P(('lat', 'lon')), may hold values from 0 to 128, as said below
Outputs:
- density_grad: float32 [128, 256, 4096], P('coh', 'lat', 'lon')
- recruit_grad: float32 [256, 4096], P('lat', 'lon')
The draws below stay inside these ranges and needn't reach their ends.
Inputs may be any that keep to these rules, and one draw needn't show every extreme that they name: `fleet_east_piece`: among the rows of one device, at most 3 name the same longitude tile, and some longitude tile is named by exactly 3 of them. `fleet_age_bounds`: in every row the first entry is below the second.
All inputs are finite; a program needn't handle non-finite values. No bound on the sum of `marine_indicator` on one device may be relied on, other than what follows from the above.
Results may differ from the reference program's by a relative error of at most 0.0003.
Values sent between devices are 32-bit elements; how exact they have to be, the bound alone decides.
A program may use at most 64 MiB of HBM per device.

```python
import math
import jax
import jax.numpy as jnp
import numpy as np
from jax import lax

AGE_CLASSES = 128
CY = 64
CX = 256
TIME_PERIODS = 2
BY = 16
BX = 32
ROWS_DEV = 32
FLEET = 2048
CAP = 3
BLOCKS = 32
NORTH_SOUTH_LINES = 256
EAST_WEST_LINES = 4096
N_LAT = 4
N_LON = 16


def draw_fleet_age_bounds(key, part):
    picks = jax.random.randint(jax.random.fold_in(key, 7), (FLEET, 2), 0, AGE_CLASSES)
    lower = jnp.minimum(picks[:, 0], picks[:, 1])
    upper = jnp.maximum(picks[:, 0], picks[:, 1]) + 1
    return jnp.stack([lower, upper], axis=1).astype(jnp.int32)


def set_ends(drawn, stream_key, low, high):
    shape = drawn.shape
    spot = [jax.random.randint(jax.random.fold_in(stream_key, axis), (), 0, shape[axis]) for axis in range(len(shape))]
    drawn = drawn.at[tuple(spot)].set(low)
    longest = shape.index(max(shape))
    spot[longest] = (spot[longest] + 1) % shape[longest]
    return drawn.at[tuple(spot)].set(high)


def block_levels(rng, shape, pieces, smallest, largest):
    gain, own = 1.0, jax.random.fold_in(rng, 6)
    for axis_at, parts in pieces:
        draws = jnp.exp(jax.random.uniform(jax.random.fold_in(own, axis_at), (parts,), jnp.float32, smallest / len(pieces), largest / len(pieces)))
        gain = gain * jnp.repeat(draws, shape[axis_at] // parts).reshape([-1 if axis == axis_at else 1 for axis in range(len(shape))])
    return gain


def deal_out(own_key, own, number, rows, number_of, top, most, lean):
    order = jax.random.permutation(own_key, number_of)
    heavy_load, common = portions_of(number_of, rows * top, most, lean, True), portions_of(number_of, rows * top, most, lean, False)
    places = jnp.arange(number_of)

    def named(tallies, rotation):
        used = int((tallies > 0).sum())
        fixed = max(1, used // 4)
        passed = fixed + (places - fixed + rotation * (used - fixed)) % max(1, number_of - fixed)
        return jnp.zeros((number_of,), jnp.int32).at[order[jnp.where(places < fixed, places, passed)]].set(jnp.asarray(tallies, jnp.int32))

    tallies = jnp.where(number % 4 == 0, named(heavy_load, number // 4), named(common, number - number // 4 - 1))
    mixed = jax.random.permutation(jax.random.fold_in(own, 3), number_of)
    giver, receiver = mixed[0:number_of // 2 * 2:2], mixed[1:number_of // 2 * 2:2]
    slack = jnp.minimum(tallies[giver] - 1, most - tallies[receiver]) // 2
    slack = jnp.where((giver == order[0]) | (receiver == order[0]) | (tallies[receiver] == 0), 0, jnp.maximum(slack, 0))
    passed = jax.random.randint(jax.random.fold_in(own, 4), (number_of // 2,), 0, 1 << 20) % (slack + 1)
    tallies = tallies.at[giver].add(-passed).at[receiver].add(passed)
    labels = jnp.searchsorted(jnp.cumsum(tallies), jnp.arange(rows * top), side="right").astype(jnp.int32)
    listing = labels.reshape(top, rows).T
    listing = listing[jax.random.permutation(jax.random.fold_in(own, 1), rows)]
    rotation = jax.random.randint(jax.random.fold_in(own, 2), (rows, 1), 0, top)
    return jnp.take_along_axis(listing, (jnp.arange(top)[None, :] + rotation) % top, axis=1)


def portions_of(amount, total, bound, lean, full):
    weights = [(1 << 20) // math.isqrt(grade ** lean) + 1 for grade in range(1, amount + 1)]
    largest = bound if full else min(bound, max(-(-total // amount), total * weights[0] // sum(weights)))
    least = 1 if total - largest >= amount - 1 else 0
    given, surplus = [largest] + [least] * (amount - 1), total - largest - least * (amount - 1)
    while surplus > 0:
        candidates = [i for i in range(1, amount) if given[i] < largest] or [i for i in range(1, amount) if given[i] < bound]
        whole, remaining = sum([weights[i] for i in candidates]), surplus
        for i in candidates:
            more = min(bound - given[i], max(1, remaining * weights[i] // whole), surplus)
            given[i] = given[i] + more
            surplus = surplus - more
    return np.array(given)


def gaussian(own_key, extent, width, reach, cuts=(), dtype=jnp.bfloat16):
    result = width * jax.random.normal(own_key, extent, jnp.float32)
    if cuts:
        result = result * block_levels(own_key, extent, cuts, -0.22, 0.18)
    return jnp.clip(result, -reach, reach).astype(dtype)


def setup_inputs(seed: int = 0) -> dict:
    splits = jax.random.split(jax.random.key(seed), 19)
    saved_period_abundance = jnp.clip(jnp.exp(math.log(2.0) - 2.9996462 * jax.random.uniform(splits[0], (TIME_PERIODS, AGE_CLASSES, NORTH_SOUTH_LINES, EAST_WEST_LINES), jnp.float32) ** block_levels(splits[0], (TIME_PERIODS, AGE_CLASSES, NORTH_SOUTH_LINES, EAST_WEST_LINES), ((1, 4), (2, 4), (3, 16)), -0.2, 0.2)), 0.099609375, 2.0).astype(jnp.bfloat16)
    final_abundance_sensitivity = gaussian(splits[1], (AGE_CLASSES, NORTH_SOUTH_LINES, EAST_WEST_LINES), 1.0, 6.0, ((0, 4), (1, 4), (2, 16)))
    prey_biomass = jnp.clip(jnp.exp(math.log(2.0) - 2.3025851 * jax.random.uniform(splits[2], (TIME_PERIODS, NORTH_SOUTH_LINES, EAST_WEST_LINES), jnp.float32) ** block_levels(splits[2], (TIME_PERIODS, NORTH_SOUTH_LINES, EAST_WEST_LINES), ((1, 4), (2, 16)), -0.2, 0.2)), 0.2, 2.0)
    water_heat_field = jnp.clip(10.0 + 20.0 * jax.random.uniform(splits[3], (TIME_PERIODS, NORTH_SOUTH_LINES, EAST_WEST_LINES), jnp.float32) ** block_levels(splits[3], (TIME_PERIODS, NORTH_SOUTH_LINES, EAST_WEST_LINES), ((1, 4), (2, 16)), -0.2, 0.2), 10.0, 30.0)
    marine_indicator = set_ends((jax.random.randint(splits[4], (NORTH_SOUTH_LINES, EAST_WEST_LINES), 0, 5) < 4).astype(jnp.int32), jax.random.fold_in(splits[4], 1), 0, 1)
    fishing_pressure = jnp.clip(jnp.exp(math.log(2.0) - 2.9957323 * jax.random.uniform(splits[5], (NORTH_SOUTH_LINES, EAST_WEST_LINES), jnp.float32) ** block_levels(splits[5], (NORTH_SOUTH_LINES, EAST_WEST_LINES), ((0, 4), (1, 16)), -0.2, 0.2)), 0.1, 2.0)
    offspring_yield = jnp.clip(jnp.exp(math.log(20.0) - 2.3025851 * jax.random.uniform(splits[6], (NORTH_SOUTH_LINES, EAST_WEST_LINES), jnp.float32) ** block_levels(splits[6], (NORTH_SOUTH_LINES, EAST_WEST_LINES), ((0, 4), (1, 16)), -0.2, 0.2)), 2.0, 20.0)
    death_fraction = jnp.clip(jnp.exp(math.log(0.5) - 3.912023 * jax.random.uniform(splits[7], (AGE_CLASSES,), jnp.float32) ** block_levels(splits[7], (AGE_CLASSES,), ((0, 4),), -0.2, 0.2)), 0.01, 0.5)
    gear_vulnerability = jnp.clip(jnp.exp(math.log(0.5) - 2.3025851 * jax.random.uniform(splits[8], (AGE_CLASSES,), jnp.float32) ** block_levels(splits[8], (AGE_CLASSES,), ((0, 4),), -0.2, 0.2)), 0.05, 0.5)
    spreading_coefficient = jnp.clip(jnp.exp(math.log(0.12) - 1.7917595 * jax.random.uniform(splits[9], (AGE_CLASSES,), jnp.float32) ** block_levels(splits[9], (AGE_CLASSES,), ((0, 4),), -0.2, 0.2)), 0.02, 0.12)
    directed_drift_rate = jnp.clip(jnp.exp(math.log(0.06) - 1.7917595 * jax.random.uniform(splits[10], (AGE_CLASSES,), jnp.float32) ** block_levels(splits[10], (AGE_CLASSES,), ((0, 4),), -0.2, 0.2)), 0.01, 0.06)
    favoured_thermal_level = jnp.clip(12.0 + 16.0 * jax.random.uniform(splits[11], (AGE_CLASSES,), jnp.float32) ** block_levels(splits[11], (AGE_CLASSES,), ((0, 4),), -0.2, 0.2), 12.0, 28.0)
    breeding_contribution = jnp.clip(jnp.exp(math.log(0.03) - 1.7917595 * jax.random.uniform(splits[12], (AGE_CLASSES,), jnp.float32) ** block_levels(splits[12], (AGE_CLASSES,), ((0, 4),), -0.2, 0.2)), 0.005, 0.03)
    landing_error_sensitivity = gaussian(splits[13], (FLEET, TIME_PERIODS, AGE_CLASSES), 1.0, 6.0, ((0, 64), (2, 4)), jnp.float32)
    fleet_east_piece_keys = jax.random.split(jax.random.fold_in(splits[14], 1), FLEET // ROWS_DEV)
    fleet_east_piece_turns = jax.random.permutation(jax.random.fold_in(splits[14], 3), FLEET // ROWS_DEV)
    fleet_east_piece = jax.vmap(lambda own, number: deal_out(jax.random.fold_in(splits[14], 2), own, number, ROWS_DEV, N_LON, 1, CAP, 2))(fleet_east_piece_keys, fleet_east_piece_turns).reshape((FLEET, 1))
    fleet_north_piece = set_ends(jax.random.randint(splits[15], (FLEET,), 0, N_LAT), jax.random.fold_in(splits[15], 1), 0, N_LAT - 1).astype(jnp.int32)
    fleet_area_patch = set_ends(jax.random.randint(splits[16], (FLEET,), 0, BLOCKS), jax.random.fold_in(splits[16], 1), 0, BLOCKS - 1).astype(jnp.int32)
    fleet_age_bounds = draw_fleet_age_bounds(jax.random.fold_in(splits[18], 71), 0)
    return {"saved_period_abundance": saved_period_abundance, "final_abundance_sensitivity": final_abundance_sensitivity, "prey_biomass": prey_biomass, "water_heat_field": water_heat_field, "marine_indicator": marine_indicator, "fishing_pressure": fishing_pressure, "offspring_yield": offspring_yield, "death_fraction": death_fraction, "gear_vulnerability": gear_vulnerability, "spreading_coefficient": spreading_coefficient, "directed_drift_rate": directed_drift_rate, "favoured_thermal_level": favoured_thermal_level, "breeding_contribution": breeding_contribution, "landing_error_sensitivity": landing_error_sensitivity, "fleet_east_piece": fleet_east_piece, "fleet_north_piece": fleet_north_piece, "fleet_area_patch": fleet_area_patch, "fleet_age_bounds": fleet_age_bounds}


thermal_tolerance_spread = 4.0
age_class_bundle = 16
highest = lax.Precision.HIGHEST


def shifted_views(values_in):
    lead = [(0, 0)] * (values_in.ndim - 2)
    padded = jnp.pad(values_in, lead + [(1, 1), (1, 1)])
    return (padded[..., :-2, 1:-1], padded[..., 2:, 1:-1], padded[..., 1:-1, 2:], padded[..., 1:-1, :-2])


def reference(saved_period_abundance, final_abundance_sensitivity, prey_biomass, water_heat_field, marine_indicator, fishing_pressure, offspring_yield, death_fraction, gear_vulnerability, spreading_coefficient, directed_drift_rate, favoured_thermal_level, breeding_contribution, landing_error_sensitivity, fleet_east_piece, fleet_north_piece, fleet_area_patch, fleet_age_bounds):
    sea_field = marine_indicator.astype(jnp.float32)
    cohort_age = jnp.arange(AGE_CLASSES).astype(jnp.int32)
    maturity = (cohort_age + 1).astype(jnp.float32) / AGE_CLASSES * breeding_contribution
    blocks_y = CY // BY
    blocks_x = CX // BX
    grid_y = NORTH_SOUTH_LINES // BY
    grid_x = EAST_WEST_LINES // BX
    block_row = fleet_north_piece * blocks_y + fleet_area_patch // blocks_x
    block_col = fleet_east_piece[:, 0] * blocks_x + fleet_area_patch % blocks_x
    place_id = block_row * grid_x + block_col
    inside = (cohort_age[None, :] >= fleet_age_bounds[:, 0:1]) & (cohort_age[None, :] < fleet_age_bounds[:, 1:2])
    masked = landing_error_sensitivity * inside[:, None, :].astype(jnp.float32)
    onehot = (jnp.arange(grid_y * grid_x).astype(jnp.int32)[:, None] == place_id[None, :]).astype(jnp.float32)
    block_values = jnp.dot(onehot, masked.reshape(FLEET, TIME_PERIODS * AGE_CLASSES), precision=highest)
    block_values = block_values.reshape(grid_y, grid_x, TIME_PERIODS, AGE_CLASSES).transpose(2, 3, 0, 1)
    adjoint = final_abundance_sensitivity.astype(jnp.float32)
    grad_recruit = jnp.zeros((NORTH_SOUTH_LINES, EAST_WEST_LINES), jnp.float32)
    sea_views = shifted_views(sea_field)
    for period_counter in range(TIME_PERIODS - 1, -1, -1):
        density = saved_period_abundance[period_counter].astype(jnp.float32)
        spawning = jnp.tensordot(maturity, density, axes=1, precision=highest)
        first_plane = adjoint[0]
        ratio = 1.0 / (1.0 + spawning)
        recruit_term = first_plane * sea_field * offspring_yield * ratio * ratio
        padded_adj = jnp.concatenate([adjoint, jnp.zeros((1, NORTH_SOUTH_LINES, EAST_WEST_LINES), jnp.float32)], axis=0)
        forage_now = prey_biomass[period_counter]
        present_thermal_field = water_heat_field[period_counter]
        catch_now = block_values[period_counter]

        def group_step(starting_offset):
            later = lax.dynamic_slice_in_dim(padded_adj, starting_offset + 1, age_class_bundle, 0)
            rate_kappa = lax.dynamic_slice_in_dim(spreading_coefficient, starting_offset, age_class_bundle)[:, None, None]
            rate_taxis = lax.dynamic_slice_in_dim(directed_drift_rate, starting_offset, age_class_bundle)[:, None, None]
            mort_part = lax.dynamic_slice_in_dim(death_fraction, starting_offset, age_class_bundle)[:, None, None]
            select_part = lax.dynamic_slice_in_dim(gear_vulnerability, starting_offset, age_class_bundle)[:, None, None]
            ideal_thermal = lax.dynamic_slice_in_dim(favoured_thermal_level, starting_offset, age_class_bundle)[:, None, None]
            mature_part = lax.dynamic_slice_in_dim(maturity, starting_offset, age_class_bundle)[:, None, None]
            thermal_departure = (present_thermal_field[None] - ideal_thermal) / thermal_tolerance_spread
            habitat = sea_field * forage_now / (1.0 + thermal_departure * thermal_departure)
            hab_views = shifted_views(habitat)
            adj_views = shifted_views(later)
            outflow = jnp.zeros_like(later)
            for sea_next, hab_next, adj_next in zip(sea_views, hab_views, adj_views):
                flow_rate = sea_field * sea_next * (rate_kappa + jnp.maximum(rate_taxis * (hab_next - habitat), 0.0))
                outflow = outflow + flow_rate * (later - adj_next)
            after_move = later - outflow
            survive = jnp.exp(-mort_part - select_part * fishing_pressure[None])
            caught = lax.dynamic_slice_in_dim(catch_now, starting_offset, age_class_bundle, 0)
            caught = jnp.repeat(jnp.repeat(caught, BY, axis=1), BX, axis=2)
            return survive * after_move + recruit_term[None] * mature_part + select_part * fishing_pressure[None] * caught

        begins = jnp.arange(AGE_CLASSES // age_class_bundle).astype(jnp.int32) * age_class_bundle
        adjoint = lax.map(group_step, begins).reshape(AGE_CLASSES, NORTH_SOUTH_LINES, EAST_WEST_LINES)
        grad_recruit = grad_recruit + first_plane * sea_field * spawning * ratio
    return adjoint, grad_recruit
```

```python
import functools
import jax
import jax.numpy as jnp
from jax import lax
from jax.experimental import pallas as pl
from jax.experimental.pallas import tpu as pltpu
from jax.sharding import PartitionSpec as P

MESH = pl.DeviceIdType.MESH
HIGHEST = lax.Precision.HIGHEST
F32 = jnp.float32
I32 = jnp.int32

AGES = 32
ROWS = 64
LANES = 128
BY = 16
SLOTS = 8
CODE = 64
TOP = 8
FIRST_AGE = 8
FIELD_LANE = 66


def iota(shape, dim):
    return lax.broadcasted_iota(I32, shape, dim)


def as_column(row):
    n = row.shape[1]
    eye = iota((n, n), 0) == iota((n, n), 1)
    return jnp.sum(jnp.where(eye, jnp.broadcast_to(row, (n, n)), 0.0), axis=1, keepdims=True)


def as_row(column):
    n = column.shape[0]
    eye = iota((n, n), 0) == iota((n, n), 1)
    return jnp.sum(jnp.where(eye, jnp.broadcast_to(column, (n, n)), 0.0), axis=0, keepdims=True)


def kernel(
    sizes,
    saved, final, prey, heat, sea_in, fish, offspring,
    death, gear, spread, drift, level, breed,
    gear_v, spread_v, drift_v, level_v,
    landing, east, north, patch, bounds,
    out, grad,
    saved_v, final_v, adj1, adj0, rest, surv, hab,
    forage, warm, sea, open_e, open_s, rec,
    row_n1, row_s1, row_n0, row_s0,
    halo_n1, halo_s1, halo_n0, halo_s0,
    diag_n1, diag_s1, diag_n0, diag_s0,
    col1, col0, col_w1, col_e1, col_w0, col_e0,
    dcol_w1, dcol_e1, dcol_w0, dcol_e0,
    fix_col, fix_n, fix_s,
    first1, first0, spawn, spawn_in,
    catch_v, catch_out, catch_in, fold_out, fold_in, blocks,
    local_sem, send_sem, recv_sem,
):
    n_coh, n_lat, n_lon = sizes
    c, i, j = lax.axis_index("coh"), lax.axis_index("lat"), lax.axis_index("lon")
    c_up, c_dn = lax.rem(c + 1, n_coh), lax.rem(c + n_coh - 1, n_coh)
    i_up, i_dn = lax.rem(i + 1, n_lat), lax.rem(i + n_lat - 1, n_lat)
    j_up, j_dn = lax.rem(j + 1, n_lon), lax.rem(j + n_lon - 1, n_lon)
    total_ages = AGES * n_coh

    def at(cc, ii, jj):
        return {"coh": cc, "lat": ii, "lon": jj}

    load_final = pltpu.make_async_copy(final, final_v, local_sem.at[0])
    load_saved = [pltpu.make_async_copy(saved.at[t], saved_v.at[t], local_sem.at[1 + t]) for t in range(2)]
    load_final.start()
    load_saved[1].start()
    load_saved[0].start()

    barrier = pltpu.get_barrier_semaphore()
    partners = [at(c, i, lax.rem(j + d, n_lon)) for d in range(1, n_lon)]
    partners += [at(c, lax.rem(i + d, n_lat), j) for d in range(1, n_lat)]
    partners += [at(lax.rem(c + d, n_coh), i, j) for d in range(1, n_coh)]
    partners += [at(cc, ii, j) for cc in (c_up, c_dn) for ii in (i_up, i_dn)]
    partners += [at(cc, i, jj) for cc in (c_up, c_dn) for jj in (j_up, j_dn)]
    for partner in partners:
        pl.semaphore_signal(barrier, inc=1, device_id=partner, device_id_type=MESH)

    def remote(src, dst, k, to):
        return pltpu.make_async_remote_copy(
            src_ref=src, dst_ref=dst, send_sem=send_sem.at[k], recv_sem=recv_sem.at[k],
            device_id=to, device_id_type=MESH,
        )

    lane = iota((BY, LANES), 1)
    lane_all = iota((ROWS, LANES), 1)
    age_lane = ((lane + 1) & 127) >> 1
    age_lane_all = ((lane_all + 1) & 127) >> 1
    even_all = (lane_all & 1) == 0

    def mature(a):
        return (c * AGES + a + 1).astype(F32) * (1.0 / total_ages) * breed[a]

    east_col = east[...].astype(F32)
    east_row = as_row(east_col)
    same = jnp.broadcast_to(east_col, (32, 32)) == jnp.broadcast_to(east_row, (32, 32))
    ahead = same & (iota((32, 32), 0) < iota((32, 32), 1))
    rank_row = jnp.sum(jnp.where(ahead, 1.0, 0.0), axis=0, keepdims=True)
    slot_row = east_row * SLOTS + rank_row
    code_col = as_column((north[...] * 32 + patch[...]).astype(F32))
    cohort = c * AGES + iota((32, AGES), 1)
    inside = (cohort >= bounds[:, 0:1]) & (cohort < bounds[:, 1:2])
    catch_v[...] = jnp.broadcast_to(code_col, (32, LANES))
    catch_v[:, 0:32] = jnp.where(inside, landing[:, 0, :], 0.0)
    catch_v[:, 32:64] = jnp.where(inside, landing[:, 1, :], 0.0)
    slots = n_lon * SLOTS
    place = jnp.where(iota((slots, 32), 0).astype(F32) == jnp.broadcast_to(slot_row, (slots, 32)), 1.0, 0.0)
    placed = jnp.dot(place, catch_v[...], precision=HIGHEST, preferred_element_type=F32)
    catch_out[...] = placed.reshape(n_lon, SLOTS, LANES)
    catch_in[j] = catch_out[j]

    def halves(h):
        return slice(h * LANES, (h + 1) * LANES)

    body = slice(TOP, TOP + ROWS)
    for h in range(2):
        sea[h] = sea_in[:, halves(h)].astype(F32)
    last_lane = lane_all == LANES - 1
    sea0, sea1 = sea[0], sea[1]
    next0 = jnp.where(last_lane, pltpu.roll(sea1, LANES - 1, 1), pltpu.roll(sea0, LANES - 1, 1))
    next1 = jnp.where(last_lane, 0.0, pltpu.roll(sea1, LANES - 1, 1))
    open_e[0] = sea0 * next0
    open_e[1] = sea1 * next1
    last_row = iota((ROWS, LANES), 0) == ROWS - 1
    for h, here in enumerate((sea0, sea1)):
        below = jnp.where(last_row, 0.0, pltpu.roll(here, ROWS - 1, 0))
        open_s[h, 0:TOP, :] = jnp.zeros((TOP, LANES), F32)
        open_s[h, body, :] = here * below
        hab[h, 0:TOP, :] = jnp.zeros((TOP, LANES), F32)
        hab[h, TOP + ROWS:, :] = jnp.zeros((TOP, LANES), F32)
    for t in range(2):
        for h, here in enumerate((sea0, sea1)):
            forage[t, h] = here * prey[t, :, halves(h)]
            warm[t, h] = heat[t, :, halves(h)] * 0.25

    def field(f, h):
        if f == 4:
            return sea[h]
        return (forage, warm)[f % 2][1 - f // 2, h]

    columns = jnp.zeros((ROWS, LANES), F32)
    for h in range(2):
        row_n1[h, 0:8, :] = jnp.zeros((8, LANES), F32)
        row_s1[h, 0:8, :] = jnp.zeros((8, LANES), F32)
    for f in range(5):
        for h in range(2):
            plane = field(f, h)
            row_n1[h, f:f + 1, :] = plane[0:1]
            row_s1[h, f:f + 1, :] = plane[ROWS - 1:ROWS]
        columns = jnp.where(lane_all == FIELD_LANE + 2 * f, jnp.broadcast_to(field(f, 0)[:, 0:1], (ROWS, LANES)), columns)
        columns = jnp.where(
            lane_all == FIELD_LANE + 2 * f + 1, jnp.broadcast_to(field(f, 1)[:, LANES - 1:], (ROWS, LANES)), columns
        )
    col0[...] = jnp.zeros((ROWS, LANES), F32)

    pad = jnp.zeros((TOP, LANES), F32)

    def clear_pads(adj, a):
        for h in range(2):
            adj[a, h, 0:TOP, :] = pad
            adj[a, h, TOP + ROWS:, :] = pad

    def pick_columns(a, x0, x1):
        width = iota(x0.shape, 1)
        edges = jnp.where(width == 0, x0, x1)
        return ((width + 1) & 127) >> 1 == a, pltpu.roll(edges, 2 * a, 1)

    load_final.wait()

    def unpack(a, columns):
        x = final_v[a].astype(F32)
        x0, x1 = x[:, :LANES], x[:, LANES:]
        clear_pads(adj1, a)
        clear_pads(adj0, a)
        for h, xh in enumerate((x0, x1)):
            adj1[a, h, body, :] = xh
            row_n1[h, pl.ds(FIRST_AGE + a, 1), :] = xh[0:1]
            row_s1[h, pl.ds(FIRST_AGE + a, 1), :] = xh[ROWS - 1:]
        mine, moved = pick_columns(a, x0, x1)
        return jnp.where(mine, moved, columns)

    col1[...] = lax.fori_loop(0, AGES, unpack, columns)
    clear_pads(adj1, AGES)
    clear_pads(adj0, AGES)

    def spawn_part(t):
        def add(a, total):
            return total + mature(a) * saved_v[t, a].astype(F32)

        total = lax.fori_loop(0, AGES, add, jnp.zeros((ROWS, 2 * LANES), F32))
        for h in range(2):
            spawn[t, h] = total[:, halves(h)]

    load_saved[1].wait()
    spawn_part(1)

    pl.semaphore_wait(barrier, len(partners))

    catch_sends = [
        remote(catch_out.at[lax.rem(j + d, n_lon)], catch_in.at[j], d, at(c, i, lax.rem(j + d, n_lon)))
        for d in range(1, n_lon)
    ]
    for copy in catch_sends:
        copy.start()

    k_fold, k_spawn, k_month = 16, 20, 28

    def spawn_copies(t):
        return [
            remote(spawn.at[t], spawn_in.at[t, d - 1], k_spawn + 4 * t + d, at(lax.rem(c + d, n_coh), i, j))
            for d in range(1, n_coh)
        ]

    def month_copies(t):
        k = k_month + 12 * (1 - t)
        adj = (adj0, adj1)[t]
        col = (col0, col1)[t]
        span = slice(0, 40) if t == 1 else slice(FIRST_AGE, 40)
        row_n, row_s = ((row_n0, row_s0), (row_n1, row_s1))[t]
        halo_n, halo_s = ((halo_n0, halo_s0), (halo_n1, halo_s1))[t]
        diag_n, diag_s = ((diag_n0, diag_s0), (diag_n1, diag_s1))[t]
        col_w, col_e = ((col_w0, col_e0), (col_w1, col_e1))[t]
        dcol_w, dcol_e = ((dcol_w0, dcol_e0), (dcol_w1, dcol_e1))[t]
        first = (first0, first1)[t]
        side = [
            remote(row_n.at[:, span, :], halo_s.at[:, span, :], k, at(c, i_dn, j)),
            remote(row_s.at[:, span, :], halo_n.at[:, span, :], k + 1, at(c, i_up, j)),
            remote(col, col_e, k + 4, at(c, i, j_dn)),
            remote(col, col_w, k + 5, at(c, i, j_up)),
        ]
        younger = [
            remote(adj.at[0, :, body, :], adj.at[AGES, :, body, :], k + 8, at(c_dn, i, j)),
            remote(adj.at[0, :, TOP:TOP + 8, :], diag_s, k + 2, at(c_dn, i_dn, j)),
            remote(adj.at[0, :, TOP + ROWS - 8:TOP + ROWS, :], diag_n, k + 3, at(c_dn, i_up, j)),
            remote(col, dcol_e, k + 6, at(c_dn, i, j_dn)),
            remote(col, dcol_w, k + 7, at(c_dn, i, j_up)),
        ]
        root = [remote(adj.at[0, :, body, :], first, k + 8 + d, at(d, i, j)) for d in range(1, n_coh)]
        return side, younger, root

    def start_month(t):
        side, younger, root = month_copies(t)
        adj, first = (adj0, adj1)[t], (first0, first1)[t]

        @pl.when(c > 0)
        def _():
            younger[0].start()

        @pl.when(c == 0)
        def _():
            for copy in root:
                copy.start()
            for h in range(2):
                first[h] = adj[0, h, body, :]

        for copy in side:
            copy.start()

        @pl.when(c > 0)
        def _():
            for copy in younger[1:]:
                copy.start()

    start_month(1)
    for copy in spawn_copies(1):
        copy.start()
    load_saved[0].wait()
    spawn_part(0)
    for copy in spawn_copies(0):
        copy.start()

    def interior(t, adj, a):
        spread_a, drift_a, level_a = spread[a], drift[a], level[a] * 0.25
        for h in range(2):
            for r in range(0, ROWS, BY):
                rows = slice(r, r + BY)
                q = warm[t, h, rows, :] - level_a
                hab[h, TOP + r:TOP + r + BY, :] = forage[t, h, rows, :] * drift_a / (1.0 + q * q)
                if t == 1:
                    surv[a, h, rows, :] = jnp.exp(-death[a] - gear[a] * fish[rows, halves(h)])
        for r in range(0, ROWS, BY):
            rows = slice(r, r + BY)
            mid, up, dn = (slice(TOP + r + s, TOP + r + s + BY) for s in (0, -1, 1))
            h0, h1 = hab[0, mid, :], hab[1, mid, :]
            l0, l1 = adj[a + 1, 0, mid, :], adj[a + 1, 1, mid, :]
            turn = LANES - 1
            hr1, lr1 = pltpu.roll(h1, turn, 1), pltpu.roll(l1, turn, 1)
            hr0 = jnp.where(lane == turn, hr1, pltpu.roll(h0, turn, 1))
            lr0 = jnp.where(lane == turn, lr1, pltpu.roll(l0, turn, 1))
            kept, given = [], []
            for h, hh, ll, hr, lr in ((0, h0, l0, hr0, lr0), (1, h1, l1, hr1, lr1)):
                g = hr - hh
                k = jnp.maximum(g, 0.0) + spread_a
                o = open_e[h, rows, :] * (ll - lr)
                y = ll - k * o
                given.append((k - g) * o)
                for shift, gate in ((up, up), (dn, mid)):
                    k = jnp.maximum(hab[h, shift, :] - hh, 0.0) + spread_a
                    y = y - k * (open_s[h, gate, :] * (ll - adj[a + 1, h, shift, :]))
                kept.append(y)
            m0, m1 = pltpu.roll(given[0], 1, 1), pltpu.roll(given[1], 1, 1)
            rest[a, 0, rows, :] = kept[0] + jnp.where(lane == 0, m1, m0)
            rest[a, 1, rows, :] = kept[1] + jnp.where(lane == 0, m0, m1)

    def interiors(t, lo, hi):
        adj = (adj0, adj1)[t]

        def step(a, carry):
            interior(t, adj, a)
            return carry

        lax.fori_loop(lo, hi, step, 0)

    age_of = iota((AGES, LANES), 0)
    lane_age = ((iota((AGES, LANES), 1) + 1) & 127) >> 1

    def by_row(v):
        return as_column(v[...])

    def by_lane(v):
        wide = jnp.broadcast_to(by_row(v), (AGES, LANES))
        return jnp.sum(jnp.where(age_of == lane_age, wide, 0.0), axis=0, keepdims=True)

    north_open = jnp.where(i > 0, 1.0, 0.0)
    south_open = jnp.where(i < n_lat - 1, 1.0, 0.0)
    west_open = jnp.where(j > 0, 1.0, 0.0)
    east_open = jnp.where(j < n_lon - 1, 1.0, 0.0)

    def edges(t):
        adj = (adj0, adj1)[t]
        side, younger, root = month_copies(t)
        halo_n, halo_s = ((halo_n0, halo_s0), (halo_n1, halo_s1))[t]
        row_n, row_s = ((row_n0, row_s0), (row_n1, row_s1))[t]
        diag_n, diag_s = ((diag_n0, diag_s0), (diag_n1, diag_s1))[t]
        col = (col0, col1)[t]
        col_w, col_e = ((col_w0, col_e0), (col_w1, col_e1))[t]
        dcol_w, dcol_e = ((dcol_w0, dcol_e0), (dcol_w1, dcol_e1))[t]
        for copy in side:
            copy.wait_recv()

        @pl.when(c < n_coh - 1)
        def _():
            for copy in younger[1:]:
                copy.wait_recv()

        @pl.when(c == n_coh - 1)
        def _():
            diag_n[...] = jnp.zeros_like(diag_n)
            diag_s[...] = jnp.zeros_like(diag_s)
            dcol_w[...] = jnp.zeros_like(dcol_w)
            dcol_e[...] = jnp.zeros_like(dcol_e)

        past = FIRST_AGE + AGES
        for h in range(2):
            row_n[h, past:past + 1, :] = adj[AGES, h, TOP:TOP + 1, :]
            row_s[h, past:past + 1, :] = adj[AGES, h, TOP + ROWS - 1:TOP + ROWS, :]
            halo_n[h, past:past + 1, :] = diag_n[h, 7:8, :]
            halo_s[h, past:past + 1, :] = diag_s[h, 0:1, :]
        later = slice(FIRST_AGE + 1, FIRST_AGE + 1 + AGES)
        f = 2 * (1 - t)
        spread_r, drift_r, level_r = (
            jnp.broadcast_to(x, (AGES, LANES)) for x in (by_row(spread_v), by_row(drift_v), by_row(level_v) * 0.25)
        )
        for own, halo, own1, halo1, gate, fix in (
            (row_n, halo_n, row_n1, halo_n1, north_open, fix_n),
            (row_s, halo_s, row_s1, halo_s1, south_open, fix_s),
        ):
            for h in range(2):
                def habitat(buf):
                    q = buf[h, f + 1:f + 2, :] - level_r
                    return buf[h, f:f + 1, :] * drift_r / (1.0 + q * q)

                passage = own1[h, 4:5, :] * halo1[h, 4:5, :] * gate
                k = spread_r + jnp.maximum(habitat(halo1) - habitat(own1), 0.0)
                fix[h] = passage * k * (own[h, later, :] - halo[h, later, :])

        def both(own_w, own_e):
            wide = (ROWS, LANES)
            return jnp.where(even_all, jnp.broadcast_to(own_w, wide), jnp.broadcast_to(own_e, wide))

        def own_field(f):
            return both(field(f, 0)[:, 0:1], field(f, 1)[:, LANES - 1:])

        def halo_field(f):
            spot = FIELD_LANE + 2 * f
            return both(col_w1[:, spot + 1:spot + 2], col_e1[:, spot:spot + 1])

        spread_l, drift_l, level_l = (by_lane(x) for x in (spread_v, drift_v, level_v))

        def habitat_columns(get):
            q = get(f + 1) - level_l * 0.25
            return get(f) * drift_l / (1.0 + q * q)

        passage = own_field(4) * halo_field(4) * jnp.where(even_all, west_open, east_open)
        mine, moved = pick_columns(AGES, adj[AGES, 0, body, :], adj[AGES, 1, body, :])
        own = pltpu.roll(jnp.where(mine, moved, col[...]), LANES - 2, 1)
        other = jnp.where(even_all, pltpu.roll(col_w[...], LANES - 1, 1), pltpu.roll(col_e[...], LANES - 3, 1))
        other = jnp.where(lane_all == 62, pltpu.roll(dcol_w[...], 63, 1), other)
        other = jnp.where(lane_all == 61, pltpu.roll(dcol_e[...], 61, 1), other)
        k = spread_l + jnp.maximum(habitat_columns(halo_field) - habitat_columns(own_field), 0.0)
        fix_col[...] = passage * k * (own - other)

    def finish(t):
        adj_next = adj0
        place = t * AGES

        def step(a, carry):
            scale = mature(a)
            for h in range(2):
                rest[a, h, 0:1, :] = rest[a, h, 0:1, :] - fix_n[h, pl.ds(a, 1), :]
                rest[a, h, ROWS - 1:ROWS, :] = rest[a, h, ROWS - 1:ROWS, :] - fix_s[h, pl.ds(a, 1), :]
            for b in range(ROWS // BY):
                rows = slice(b * BY, (b + 1) * BY)
                turned = pltpu.roll(fix_col[rows, :], (LANES - 2 * a) & (LANES - 1), 1)
                made = []
                for h in range(2):
                    spot = (0, LANES - 1)[h]
                    moved = rest[a, h, rows, :] - jnp.where(lane == spot, turned, 0.0)
                    caught = jnp.broadcast_to(blocks[2 * b + h, pl.ds(place + a, 1), :], (BY, LANES))
                    made.append(
                        surv[a, h, rows, :] * moved + rec[h, rows, :] * scale + fish[rows, halves(h)] * caught
                    )
                if t == 1:
                    for h in range(2):
                        adj_next[a, h, TOP + b * BY:TOP + (b + 1) * BY, :] = made[h]
                        if b == 0:
                            row_n0[h, pl.ds(FIRST_AGE + a, 1), :] = made[h][0:1]
                        if b == ROWS // BY - 1:
                            row_s0[h, pl.ds(FIRST_AGE + a, 1), :] = made[h][BY - 1:]
                    mine, moved = pick_columns(a, made[0], made[1])
                    col0[rows, :] = jnp.where(mine, moved, col0[rows, :])
                else:
                    for h in range(2):
                        out[a, rows, halves(h)] = made[h]
            return carry

        lax.fori_loop(0, AGES, step, 0)

    def last_cohort(t):
        adj = (adj0, adj1)[t]
        side, younger, root = month_copies(t)

        @pl.when(c < n_coh - 1)
        def _():
            younger[0].wait_recv()

        @pl.when(c == n_coh - 1)
        def _():
            for h in range(2):
                adj[AGES, h, body, :] = jnp.zeros((ROWS, LANES), F32)

        interiors(t, AGES - 1, AGES)

    def recruit(t):
        first = (first0, first1)[t]
        side, younger, root = month_copies(t)
        for d in range(1, n_coh):
            @pl.when(c == d)
            def _():
                root[d - 1].wait_recv()
        for copy in spawn_copies(t):
            copy.wait_recv()
        for h in range(2):
            total = spawn[t, h]
            for d in range(1, n_coh):
                total = total + spawn_in[t, d - 1, h]
            ratio = 1.0 / (1.0 + total)
            base = first[h] * sea[h]
            rec[h] = base * offspring[:, halves(h)] * ratio * ratio
            gain = base * total * ratio
            if t == 1:
                grad[:, halves(h)] = gain
            else:
                grad[:, halves(h)] = grad[:, halves(h)] + gain

    fold_sends = [
        remote(fold_out.at[lax.rem(i + d, n_lat)], fold_in.at[i], k_fold + d, at(c, lax.rem(i + d, n_lat), j))
        for d in range(1, n_lat)
    ]

    interiors(1, 0, AGES // 2)
    for copy in catch_sends:
        copy.wait_recv()
    got = catch_in[...].reshape(slots, LANES)
    codes = n_lat * 32
    code_row = as_row(got[:, CODE:CODE + 1])
    pick = jnp.where(iota((codes, slots), 0).astype(F32) == jnp.broadcast_to(code_row, (codes, slots)), 1.0, 0.0)
    folded = jnp.dot(pick, got, precision=HIGHEST, preferred_element_type=F32)
    fold_out[...] = folded.reshape(n_lat, 32, LANES)
    fold_in[i] = fold_out[i]
    for copy in fold_sends:
        copy.start()
    interiors(1, AGES // 2, AGES - 1)
    last_cohort(1)
    edges(1)
    recruit(1)
    for copy in fold_sends:
        copy.wait_recv()
    block = fold_in[0]
    for d in range(1, n_lat):
        block = block + fold_in[d]
    cells = 2 * LANES * (ROWS // BY)
    widen = jnp.where(iota((32, cells), 0) == iota((32, cells), 1) >> 5, 1.0, 0.0)
    planes = lax.dot_general(block, widen, (((0,), (0,)), ((), ())), precision=HIGHEST, preferred_element_type=F32)
    gear_r = jnp.broadcast_to(by_row(gear_v), (AGES, LANES))
    for b in range(cells // LANES):
        for t in range(2):
            blocks[b, t * AGES:(t + 1) * AGES, :] = (
                planes[t * AGES:(t + 1) * AGES, b * LANES:(b + 1) * LANES] * gear_r
            )
    finish(1)
    start_month(0)
    interiors(0, 0, AGES - 1)
    last_cohort(0)
    edges(0)
    recruit(0)
    finish(0)

    for copy in catch_sends + fold_sends + spawn_copies(1) + spawn_copies(0):
        copy.wait_send()
    for t in range(2):
        side, younger, root = month_copies(t)
        for copy in side:
            copy.wait_send()

        @pl.when(c > 0)
        def _():
            for copy in younger:
                copy.wait_send()

        @pl.when(c == 0)
        def _():
            for copy in root:
                copy.wait_send()


def shards(
    sizes,
    saved, final, prey, heat, sea, fish, offspring,
    death, gear, spread, drift, level, breed,
    landing, east, north, patch, bounds,
):
    n_coh, n_lat, n_lon = sizes
    vmem = pl.BlockSpec(memory_space=pltpu.VMEM)
    smem = pl.BlockSpec(memory_space=pltpu.SMEM)
    anywhere = pl.BlockSpec(memory_space=pl.ANY)
    plane = (2, ROWS, LANES)
    padded = (AGES + 1, 2, ROWS + 2 * TOP, LANES)
    edge_rows, tile, column = (2, 48, LANES), (2, 8, LANES), (ROWS, LANES)

    def f32(shape):
        return pltpu.VMEM(shape, F32)

    scratch = [
        pltpu.VMEM((2, AGES, ROWS, 2 * LANES), jnp.bfloat16),
        pltpu.VMEM((AGES, ROWS, 2 * LANES), jnp.bfloat16),
        f32(padded), f32(padded),
        f32((AGES, *plane)), f32((AGES, *plane)),
        f32((2, ROWS + 2 * TOP, LANES)),
        f32((2, *plane)), f32((2, *plane)),
        f32(plane), f32(plane), f32((2, ROWS + 2 * TOP, LANES)), f32(plane),
        *[f32(edge_rows) for _ in range(8)],
        *[f32(tile) for _ in range(4)],
        *[f32(column) for _ in range(10)],
        f32(column), f32((2, AGES, LANES)), f32((2, AGES, LANES)),
        f32(plane), f32(plane),
        f32((2, *plane)), f32((2, n_coh - 1, *plane)),
        f32((32, LANES)), f32((n_lon, SLOTS, LANES)), f32((n_lon, SLOTS, LANES)),
        f32((n_lat, 32, LANES)), f32((n_lat, 32, LANES)),
        f32((2 * ROWS // BY, 2 * AGES, LANES)),
        pltpu.SemaphoreType.DMA((3,)),
        pltpu.SemaphoreType.DMA((52,)),
        pltpu.SemaphoreType.DMA((52,)),
    ]
    return pl.pallas_call(
        functools.partial(kernel, sizes),
        out_shape=(
            jax.ShapeDtypeStruct((AGES, ROWS, 2 * LANES), F32),
            jax.ShapeDtypeStruct((ROWS, 2 * LANES), F32),
        ),
        in_specs=[anywhere] * 2 + [vmem] * 5 + [smem] * 6 + [vmem] * 9,
        out_specs=(vmem, vmem),
        scratch_shapes=scratch,
        compiler_params=pltpu.CompilerParams(
            collective_id=0, has_side_effects=True, vmem_limit_bytes=48 * 1024 * 1024
        ),
    )(
        saved, final, prey, heat, sea, fish, offspring,
        death, gear, spread, drift, level, breed,
        gear.reshape(1, -1), spread.reshape(1, -1), drift.reshape(1, -1), level.reshape(1, -1),
        landing, east, north.reshape(1, -1), patch.reshape(1, -1), bounds,
    )


def solution(mesh):
    sizes = tuple(mesh.shape[axis] for axis in ("coh", "lat", "lon"))
    tile = P("lat", "lon")
    months = P(None, "lat", "lon")
    rows = ("lat", "lon")
    in_specs = (
        P(None, "coh", "lat", "lon"), P("coh", "lat", "lon"), months, months, tile, tile, tile,
        *[P("coh")] * 6,
        P(rows, None, "coh"), P(rows, None), P(rows), P(rows), P(rows, None),
    )
    out_specs = (P("coh", "lat", "lon"), tile)
    return jax.shard_map(
        functools.partial(shards, sizes), mesh=mesh, in_specs=in_specs, out_specs=out_specs, check_vma=False
    )
```

```python
import functools
import itertools
import jax
import jax.numpy as jnp
from jax import lax
from jax.experimental import pallas as pl
from jax.experimental.pallas import tpu as pltpu
from jax.sharding import PartitionSpec as P

LOG2E = 1.4426950408889634
MESH = pl.DeviceIdType.MESH
F32 = jnp.float32
I32 = jnp.int32

AGES = 32
ROWS = 64
LANES = 128
BY = 16
SLOTS = 8
CODE = 64
PAD = 8
FIRST_AGE = 8
FIELD_LANE = 66
GROUP = 8
GIVEN = 20


def iota(shape, dim):
    return lax.broadcasted_iota(I32, shape, dim)


def as_column(row):
    n = row.shape[1]
    eye = iota((n, n), 0) == iota((n, n), 1)
    return jnp.sum(jnp.where(eye, jnp.broadcast_to(row, (n, n)), 0.0), axis=1, keepdims=True)


def as_row(column):
    n = column.shape[0]
    eye = iota((n, n), 0) == iota((n, n), 1)
    return jnp.sum(jnp.where(eye, jnp.broadcast_to(column, (n, n)), 0.0), axis=0, keepdims=True)


def parts(x):
    high = x.astype(jnp.bfloat16)
    left = x - high.astype(F32)
    mid = left.astype(jnp.bfloat16)
    return high, mid, (left - mid.astype(F32)).astype(jnp.bfloat16)


def selected(onehot, x):
    flags = onehot.astype(jnp.bfloat16)
    return sum(jnp.dot(flags, part, preferred_element_type=F32) for part in parts(x))


def repeat(lo, hi, width, fn, carry):
    def step(n, carry):
        for m in range(width):
            carry = fn(lo + n * width + m, carry)
        return carry

    count = (hi - lo) // width
    if count:
        carry = lax.fori_loop(0, count, step, carry)
    for a in range(lo + count * width, hi):
        carry = fn(a, carry)
    return carry


def halves(h):
    return slice(h * LANES, (h + 1) * LANES)


def finished(b, a, rest, fix_col, fix_n, fix_s, blocks, place, recruits, catches, consts):
    rows = slice(b * BY, (b + 1) * BY)
    lane, row = iota((BY, LANES), 1), iota((BY, LANES), 0)
    turned = pltpu.roll(fix_col[rows, :], (LANES - 2 * a) & (LANES - 1), 1)
    made = []
    loss, share, scale = (jnp.broadcast_to(consts[n, pl.ds(a, 1), :], (BY, LANES)) for n in range(3))
    for h in range(2):
        moved = rest[a, h, rows, :] - jnp.where(lane == (0, LANES - 1)[h], turned, 0.0)
        for at, end, fix in ((0, 0, fix_n), (ROWS // BY - 1, BY - 1, fix_s)):
            if b == at:
                edge = jnp.broadcast_to(fix[h, pl.ds(a, 1), :], (BY, LANES))
                moved = moved - jnp.where(row == end, edge, 0.0)
        caught = jnp.broadcast_to(blocks[2 * b + h, pl.ds(place + a, 1), :], (BY, LANES))
        survive = jnp.exp2(loss - share * catches[h])
        made.append(survive * moved + recruits[h] * scale + catches[h] * caught)
    return made


def kernel(sizes, saved, final, *refs):
    given, made, scratch = refs[:GIVEN], refs[GIVEN:GIVEN + 9], refs[GIVEN + 9:]
    local, scratch = scratch[:GIVEN], scratch[GIVEN:]
    (
        prey, heat, sea_in, fish, offspring,
        spread, drift, level, breed,
        gear_v, spread_v, drift_v, level_v, death_v, breed_v,
        landing, east, north, patch, bounds,
    ) = local
    (
        saved_v, final_v, adj1, adj0, rest1, hab, flow,
        forage, warm, sea, open_e, open_s, rec1,
        row_n1, row_s1, row_n0, row_s0,
        halo_n1, halo_s1, halo_n0, halo_s0,
        diag_n1, diag_s1, diag_n0, diag_s0,
        col1, col0, col_w1, col_e1, col_w0, col_e0,
        dcol_w1, dcol_e1, dcol_w0, dcol_e0,
        fix_col1, fix_n1, fix_s1,
        first1, first0, spawn, spawn_a, spawn_s, spawn_b,
        catch_v, catch_out, catch_in, fold_out, fold_in, blocks1,
        local_sem, send_sem, recv_sem,
    ) = scratch
    rest, fix_col, fix_n, fix_s, rec, blocks, consts, fish_out, grad = made
    n_coh, n_lat, n_lon = sizes
    c, i, j = lax.axis_index("coh"), lax.axis_index("lat"), lax.axis_index("lon")
    c_up, c_dn = lax.rem(c + 1, n_coh), lax.rem(c + n_coh - 1, n_coh)
    i_up, i_dn = lax.rem(i + 1, n_lat), lax.rem(i + n_lat - 1, n_lat)
    j_up, j_dn = lax.rem(j + 1, n_lon), lax.rem(j + n_lon - 1, n_lon)
    total_ages = AGES * n_coh

    def at(cc, ii, jj):
        return {"coh": cc, "lat": ii, "lon": jj}

    load_final = pltpu.make_async_copy(final, final_v, local_sem.at[0])
    load_saved = [pltpu.make_async_copy(saved.at[t], saved_v.at[t], local_sem.at[1 + t]) for t in range(2)]
    fetches = [pltpu.make_async_copy(src, dst, local_sem.at[3 + n]) for n, (src, dst) in enumerate(zip(given, local))]
    for copy in fetches[15:] + fetches[:3]:
        copy.start()
    load_final.start()
    for copy in fetches[3:15] + [load_saved[1], load_saved[0]]:
        copy.start()

    barrier = pltpu.get_barrier_semaphore()
    partners = [at(c, i, lax.rem(j + d, n_lon)) for d in range(1, n_lon)]
    partners += [at(c, lax.rem(i + d, n_lat), j) for d in range(1, n_lat)]
    partners += [at(lax.rem(c + d, n_coh), i, j) for d in range(1, n_coh)]
    partners += [at(cc, ii, j) for cc in (c_up, c_dn) for ii in (i_up, i_dn)]
    partners += [at(cc, i, jj) for cc in (c_up, c_dn) for jj in (j_up, j_dn)]
    for partner in partners:
        pl.semaphore_signal(barrier, inc=1, device_id=partner, device_id_type=MESH)

    def remote(src, dst, k, to):
        return pltpu.make_async_remote_copy(
            src_ref=src, dst_ref=dst, send_sem=send_sem.at[k], recv_sem=recv_sem.at[k],
            device_id=to, device_id_type=MESH,
        )

    lane = iota((BY, LANES), 1)
    lane_all = iota((ROWS, LANES), 1)
    even_all = (lane_all & 1) == 0

    def mature(a):
        return (c * AGES + a + 1).astype(F32) * (1.0 / total_ages) * breed[a]

    for copy in fetches[15:]:
        copy.wait()
    east_row = east[...].astype(F32)
    east_col = as_column(east_row)
    same = jnp.broadcast_to(east_col, (32, 32)) == jnp.broadcast_to(east_row, (32, 32))
    ahead = same & (iota((32, 32), 0) < iota((32, 32), 1))
    rank_row = jnp.sum(jnp.where(ahead, 1.0, 0.0), axis=0, keepdims=True)
    slot_row = east_row * SLOTS + rank_row
    code_col = as_column((north[...] * 32 + patch[...]).astype(F32))
    cohort = (c * AGES + iota((32, AGES), 1)).astype(F32)
    lower, upper = (as_column(bounds[n:n + 1, :].astype(F32)) for n in range(2))
    inside = (cohort >= lower) & (cohort < upper)
    catch_v[...] = jnp.broadcast_to(code_col, (32, LANES))
    catch_v[:, 0:32] = jnp.where(inside, landing[:, 0, :], 0.0)
    catch_v[:, 32:64] = jnp.where(inside, landing[:, 1, :], 0.0)
    slots = n_lon * SLOTS
    place = jnp.where(iota((slots, 32), 0).astype(F32) == jnp.broadcast_to(slot_row, (slots, 32)), 1.0, 0.0)
    catch_out[...] = selected(place, catch_v[...]).reshape(n_lon, SLOTS, LANES)
    catch_in[j] = catch_out[j]

    pl.semaphore_wait(barrier, len(partners))

    catch_sends = [
        remote(catch_out.at[lax.rem(j + d, n_lon)], catch_in.at[j], d, at(c, i, lax.rem(j + d, n_lon)))
        for d in range(1, n_lon)
    ]
    for copy in catch_sends:
        copy.start()

    body = slice(0, ROWS)
    for copy in fetches[:3]:
        copy.wait()
    for h in range(2):
        sea[h] = sea_in[:, halves(h)].astype(F32)
    last_lane = lane_all == LANES - 1
    sea0, sea1 = sea[0], sea[1]
    turned1 = pltpu.roll(sea1, LANES - 1, 1)
    open_e[0] = sea0 * jnp.where(last_lane, turned1, pltpu.roll(sea0, LANES - 1, 1))
    open_e[1] = sea1 * jnp.where(last_lane, 0.0, turned1)
    last_row = iota((ROWS, LANES), 0) == ROWS - 1
    pad = jnp.zeros((PAD, LANES), F32)
    for h, here in enumerate((sea0, sea1)):
        open_s[h] = here * jnp.where(last_row, 0.0, pltpu.roll(here, ROWS - 1, 0))
        flow[0, h, 0:PAD, :] = pad
        flow[1, h, 0:PAD, :] = pad
        for t in range(2):
            forage[t, h] = here * prey[t, :, halves(h)]
            warm[t, h] = heat[t, :, halves(h)] * 0.25

    def field(f, h):
        if f == 4:
            return sea[h]
        return (forage, warm)[f % 2][1 - f // 2, h]

    columns = jnp.zeros((ROWS, LANES), F32)
    for h in range(2):
        row_n1[h, 0:8, :] = pad
        row_s1[h, 0:8, :] = pad
    for f in range(5):
        for h in range(2):
            plane = field(f, h)
            row_n1[h, f:f + 1, :] = plane[0:1]
            row_s1[h, f:f + 1, :] = plane[ROWS - 1:ROWS]
        columns = jnp.where(lane_all == FIELD_LANE + 2 * f, jnp.broadcast_to(field(f, 0)[:, 0:1], (ROWS, LANES)), columns)
        columns = jnp.where(
            lane_all == FIELD_LANE + 2 * f + 1, jnp.broadcast_to(field(f, 1)[:, LANES - 1:], (ROWS, LANES)), columns
        )

    def clear_pads(ref, a):
        for h in range(2):
            ref[a, h, ROWS:, :] = pad

    def pick_columns(a, x0, x1):
        width = iota(x0.shape, 1)
        edges = jnp.where(width == 0, x0, x1)
        return ((width + 1) & 127) >> 1 == a, pltpu.roll(edges, 2 * a, 1)

    load_final.wait()

    def unpack(a, columns):
        x = final_v[a].astype(F32)
        x0, x1 = x[:, :LANES], x[:, LANES:]
        clear_pads(adj1, a)
        clear_pads(adj0, a)
        for h, xh in enumerate((x0, x1)):
            adj1[a, h, body, :] = xh
            row_n1[h, pl.ds(FIRST_AGE + a, 1), :] = xh[0:1]
            row_s1[h, pl.ds(FIRST_AGE + a, 1), :] = xh[ROWS - 1:]
        mine, moved = pick_columns(a, x0, x1)
        return jnp.where(mine, moved, columns)

    col1[...] = repeat(0, AGES, 8, unpack, columns)
    clear_pads(adj1, AGES)
    clear_pads(adj0, AGES)

    k_fold, k_spawn, k_month = 16, 20, 28

    def month_copies(t):
        k = k_month + 12 * (1 - t)
        adj = (adj0, adj1)[t]
        col = (col0, col1)[t]
        span = slice(0, 40) if t == 1 else slice(FIRST_AGE, 40)
        row_n, row_s = ((row_n0, row_s0), (row_n1, row_s1))[t]
        halo_n, halo_s = ((halo_n0, halo_s0), (halo_n1, halo_s1))[t]
        diag_n, diag_s = ((diag_n0, diag_s0), (diag_n1, diag_s1))[t]
        col_w, col_e = ((col_w0, col_e0), (col_w1, col_e1))[t]
        dcol_w, dcol_e = ((dcol_w0, dcol_e0), (dcol_w1, dcol_e1))[t]
        first = (first0, first1)[t]
        side = [
            remote(row_n.at[:, span, :], halo_s.at[:, span, :], k, at(c, i_dn, j)),
            remote(row_s.at[:, span, :], halo_n.at[:, span, :], k + 1, at(c, i_up, j)),
            remote(col, col_e, k + 4, at(c, i, j_dn)),
            remote(col, col_w, k + 5, at(c, i, j_up)),
        ]
        younger = [
            remote(adj.at[0, :, body, :], adj.at[AGES, :, body, :], k + 8, at(c_dn, i, j)),
            remote(adj.at[0, :, 0:8, :], diag_s, k + 2, at(c_dn, i_dn, j)),
            remote(adj.at[0, :, ROWS - 8:ROWS, :], diag_n, k + 3, at(c_dn, i_up, j)),
            remote(col, dcol_e, k + 6, at(c_dn, i, j_dn)),
            remote(col, dcol_w, k + 7, at(c_dn, i, j_up)),
        ]
        root = [remote(adj.at[0, :, body, :], first, k + 8 + d, at(d, i, j)) for d in range(1, n_coh)]
        return side, younger, root

    def start_planes(t):
        side, younger, root = month_copies(t)
        adj, first = (adj0, adj1)[t], (first0, first1)[t]

        @pl.when(c > 0)
        def _():
            for copy in younger[:3]:
                copy.start()

        @pl.when(c == 0)
        def _():
            for copy in root:
                copy.start()
            for h in range(2):
                first[h] = adj[0, h, body, :]

    def start_edges(t):
        side, younger, root = month_copies(t)
        for copy in side:
            copy.start()

        @pl.when(c > 0)
        def _():
            for copy in younger[3:]:
                copy.start()

    start_planes(1)
    start_edges(1)

    pair = (c + 1 - 2 * lax.rem(c, 2), n_coh - 1 - c)

    def spawn_copies(t):
        one = [remote(spawn.at[t, h], spawn_a.at[t, h], k_spawn + 2 * t + h, at(pair[h], i, j)) for h in range(2)]
        two = [
            remote(spawn_s.at[t, h], spawn_b.at[t, h], k_spawn + 4 + 2 * t + h, at(pair[1 - h], i, j)) for h in range(2)
        ]
        return one, two

    def spawn_part(t):
        def add(a, total):
            return total + mature(a) * saved_v[t, a].astype(F32)

        load_saved[t].wait()
        total = repeat(0, AGES, 8, add, jnp.zeros((ROWS, 2 * LANES), F32))
        for h in range(2):
            spawn[t, h] = total[:, halves(h)]
        for copy in spawn_copies(t)[0]:
            copy.start()

    def spawn_turn(t):
        one, two = spawn_copies(t)
        for h in range(2):
            one[h].wait_recv()
            spawn_s[t, h] = spawn[t, h] + spawn_a[t, h]
            two[h].start()

    for copy in fetches[3:15]:
        copy.wait()
    spawn_part(1)
    spawn_part(0)
    fish_out[...] = fish[...]
    seniority = (c * AGES + iota((AGES, LANES), 0) + 1).astype(F32) * (1.0 / total_ages)
    consts[0] = jnp.broadcast_to(as_column(death_v[...]) * -LOG2E, (AGES, LANES))
    consts[1] = jnp.broadcast_to(as_column(gear_v[...]) * LOG2E, (AGES, LANES))
    consts[2] = jnp.broadcast_to(as_column(breed_v[...]), (AGES, LANES)) * seniority

    def habitats(t):
        def step(a, carry):
            drift_a, level_a = drift[a], level[a] * 0.25
            for h in range(2):
                for r in range(0, ROWS, BY):
                    rows = slice(r, r + BY)
                    q = warm[t, h, rows, :] - level_a
                    hab[a, h, rows, :] = forage[t, h, rows, :] * drift_a / (1.0 + q * q)
            if t == 1:
                clear_pads(hab, a)
            return carry

        repeat(0, AGES, 4, step, 0)

    def interior(adj, into, a, flow):
        spread_a = spread[a]
        turn = LANES - 1
        for r in range(0, ROWS, BY):
            mid, dn = slice(r, r + BY), slice(r + 1, r + 1 + BY)
            h0, h1 = hab[a, 0, mid, :], hab[a, 1, mid, :]
            l0, l1 = adj[a + 1, 0, mid, :], adj[a + 1, 1, mid, :]
            hr1, lr1 = pltpu.roll(h1, turn, 1), pltpu.roll(l1, turn, 1)
            hr0 = jnp.where(lane == turn, hr1, pltpu.roll(h0, turn, 1))
            lr0 = jnp.where(lane == turn, lr1, pltpu.roll(l0, turn, 1))
            kept, given = [], []
            for h, hh, ll, hr, lr in ((0, h0, l0, hr0, lr0), (1, h1, l1, hr1, lr1)):
                g = hr - hh
                k = jnp.maximum(g, 0.0) + spread_a
                o = open_e[h, mid, :] * (ll - lr)
                y = ll - k * o
                given.append((k - g) * o)
                g = hab[a, h, dn, :] - hh
                k = jnp.maximum(g, 0.0) + spread_a
                o = open_s[h, mid, :] * (ll - adj[a + 1, h, dn, :])
                flow[h, dn, :] = (k - g) * o
                kept.append(y - k * o)
            m0, m1 = pltpu.roll(given[0], 1, 1), pltpu.roll(given[1], 1, 1)
            into[a, 0, mid, :] = kept[0] + (flow[0, mid, :] + jnp.where(lane == 0, m1, m0))
            into[a, 1, mid, :] = kept[1] + (flow[1, mid, :] + jnp.where(lane == 0, m0, m1))

    def interiors(t, lo, hi):
        adj, into = (adj0, adj1)[t], (rest, rest1)[t]
        turns = itertools.count()

        def step(a, carry):
            interior(adj, into, a, flow.at[next(turns) % 2])
            return carry

        repeat(lo, hi, 2, step, 0)

    age_of = iota((AGES, LANES), 0)
    lane_age = ((iota((AGES, LANES), 1) + 1) & 127) >> 1

    def by_row(v):
        return as_column(v[...])

    def by_lane(v):
        wide = jnp.broadcast_to(by_row(v), (AGES, LANES))
        return jnp.sum(jnp.where(age_of == lane_age, wide, 0.0), axis=0, keepdims=True)

    north_open = jnp.where(i > 0, 1.0, 0.0)
    south_open = jnp.where(i < n_lat - 1, 1.0, 0.0)
    west_open = jnp.where(j > 0, 1.0, 0.0)
    east_open = jnp.where(j < n_lon - 1, 1.0, 0.0)

    def edges(t):
        adj = (adj0, adj1)[t]
        side, younger, root = month_copies(t)
        halo_n, halo_s = ((halo_n0, halo_s0), (halo_n1, halo_s1))[t]
        row_n, row_s = ((row_n0, row_s0), (row_n1, row_s1))[t]
        diag_n, diag_s = ((diag_n0, diag_s0), (diag_n1, diag_s1))[t]
        col = (col0, col1)[t]
        col_w, col_e = ((col_w0, col_e0), (col_w1, col_e1))[t]
        dcol_w, dcol_e = ((dcol_w0, dcol_e0), (dcol_w1, dcol_e1))[t]
        for copy in side:
            copy.wait_recv()

        @pl.when(c < n_coh - 1)
        def _():
            for copy in younger[1:]:
                copy.wait_recv()

        @pl.when(c == n_coh - 1)
        def _():
            diag_n[...] = jnp.zeros_like(diag_n)
            diag_s[...] = jnp.zeros_like(diag_s)
            dcol_w[...] = jnp.zeros_like(dcol_w)
            dcol_e[...] = jnp.zeros_like(dcol_e)

        past = FIRST_AGE + AGES
        for h in range(2):
            row_n[h, past:past + 1, :] = adj[AGES, h, 0:1, :]
            row_s[h, past:past + 1, :] = adj[AGES, h, ROWS - 1:ROWS, :]
            halo_n[h, past:past + 1, :] = diag_n[h, 7:8, :]
            halo_s[h, past:past + 1, :] = diag_s[h, 0:1, :]
        later = slice(FIRST_AGE + 1, FIRST_AGE + 1 + AGES)
        f = 2 * (1 - t)
        to_col, to_n, to_s = ((fix_col, fix_n, fix_s), (fix_col1, fix_n1, fix_s1))[t]
        spread_r, drift_r, level_r = (
            jnp.broadcast_to(x, (AGES, LANES)) for x in (by_row(spread_v), by_row(drift_v), by_row(level_v) * 0.25)
        )
        for own, halo, own1, halo1, gate, fix in (
            (row_n, halo_n, row_n1, halo_n1, north_open, to_n),
            (row_s, halo_s, row_s1, halo_s1, south_open, to_s),
        ):
            for h in range(2):
                def habitat(buf):
                    q = buf[h, f + 1:f + 2, :] - level_r
                    return buf[h, f:f + 1, :] * drift_r / (1.0 + q * q)

                passage = own1[h, 4:5, :] * halo1[h, 4:5, :] * gate
                k = spread_r + jnp.maximum(habitat(halo1) - habitat(own1), 0.0)
                fix[h] = passage * k * (own[h, later, :] - halo[h, later, :])

        def both(own_w, own_e):
            wide = (ROWS, LANES)
            return jnp.where(even_all, jnp.broadcast_to(own_w, wide), jnp.broadcast_to(own_e, wide))

        def own_field(f):
            return both(field(f, 0)[:, 0:1], field(f, 1)[:, LANES - 1:])

        def halo_field(f):
            spot = FIELD_LANE + 2 * f
            return both(col_w1[:, spot + 1:spot + 2], col_e1[:, spot:spot + 1])

        spread_l, drift_l, level_l = (by_lane(x) for x in (spread_v, drift_v, level_v))

        def habitat_columns(get):
            q = get(f + 1) - level_l * 0.25
            return get(f) * drift_l / (1.0 + q * q)

        passage = own_field(4) * halo_field(4) * jnp.where(even_all, west_open, east_open)
        mine, moved = pick_columns(AGES, adj[AGES, 0, body, :], adj[AGES, 1, body, :])
        own = pltpu.roll(jnp.where(mine, moved, col[...]), LANES - 2, 1)
        other = jnp.where(even_all, pltpu.roll(col_w[...], LANES - 1, 1), pltpu.roll(col_e[...], LANES - 3, 1))
        other = jnp.where(lane_all == 62, pltpu.roll(dcol_w[...], 63, 1), other)
        other = jnp.where(lane_all == 61, pltpu.roll(dcol_e[...], 61, 1), other)
        k = spread_l + jnp.maximum(habitat_columns(halo_field) - habitat_columns(own_field), 0.0)
        to_col[...] = passage * k * (own - other)

    def finish_one():
        def put(b, a, columns, recruits, catches):
            made = finished(b, a, rest1, fix_col1, fix_n1, fix_s1, blocks1, 0, recruits, catches, consts)
            for h in range(2):
                adj0[a, h, b * BY:(b + 1) * BY, :] = made[h]
                if b == 0:
                    row_n0[h, pl.ds(FIRST_AGE + a, 1), :] = made[h][0:1]
                if b == ROWS // BY - 1:
                    row_s0[h, pl.ds(FIRST_AGE + a, 1), :] = made[h][BY - 1:]
            mine, moved = pick_columns(a, made[0], made[1])
            return jnp.where(mine, moved, columns)

        def block(b):
            rows = slice(b * BY, (b + 1) * BY)
            return rows, [rec1[h, rows, :] for h in range(2)], [fish[rows, halves(h)] for h in range(2)]

        for b in range(ROWS // BY):
            rows, recruits, catches = block(b)
            col0[rows, :] = put(b, 0, jnp.zeros((BY, LANES), F32), recruits, catches)
        start_planes(0)
        for b in range(ROWS // BY):
            rows, recruits, catches = block(b)

            def step(group, columns):
                for n in range(GROUP):
                    columns = put(b, group * GROUP + n, columns, recruits, catches)
                return columns

            columns = col0[rows, :]
            for a in range(1, GROUP):
                columns = put(b, a, columns, recruits, catches)
            col0[rows, :] = lax.fori_loop(1, AGES // GROUP, step, columns)
        start_edges(0)

    def last_cohort(t):
        adj = (adj0, adj1)[t]
        side, younger, root = month_copies(t)

        @pl.when(c < n_coh - 1)
        def _():
            younger[0].wait_recv()

        @pl.when(c == n_coh - 1)
        def _():
            for h in range(2):
                adj[AGES, h, body, :] = jnp.zeros((ROWS, LANES), F32)

        interiors(t, AGES - 1, AGES)

    def recruit(t):
        first = (first0, first1)[t]
        side, younger, root = month_copies(t)
        for d in range(1, n_coh):
            @pl.when(c == d)
            def _():
                root[d - 1].wait_recv()
        two = spawn_copies(t)[1]
        for h in range(2):
            two[h].wait_recv()
            total = spawn_s[t, h] + spawn_b[t, h]
            ratio = 1.0 / (1.0 + total)
            base = first[h] * sea[h]
            (rec, rec1)[t][h] = base * offspring[:, halves(h)] * ratio * ratio
            gain = base * total * ratio
            if t == 1:
                grad[:, halves(h)] = gain
            else:
                grad[:, halves(h)] = grad[:, halves(h)] + gain

    fold_sends = [
        remote(fold_out.at[lax.rem(i + d, n_lat)], fold_in.at[i], k_fold + d, at(c, lax.rem(i + d, n_lat), j))
        for d in range(1, n_lat)
    ]

    habitats(1)
    interiors(1, 0, 14)
    for copy in catch_sends:
        copy.wait_recv()
    got = catch_in[...].reshape(slots, LANES)
    codes = n_lat * 32
    code_row = as_row(got[:, CODE:CODE + 1])
    pick = jnp.where(iota((codes, slots), 0).astype(F32) == jnp.broadcast_to(code_row, (codes, slots)), 1.0, 0.0)
    fold_out[...] = selected(pick, got).reshape(n_lat, 32, LANES)
    fold_in[i] = fold_out[i]
    for copy in fold_sends:
        copy.start()
    spawn_turn(1)
    spawn_turn(0)
    interiors(1, 14, AGES - 1)
    last_cohort(1)
    habitats(0)
    edges(1)
    recruit(1)
    for copy in fold_sends:
        copy.wait_recv()
    block = fold_in[0]
    for d in range(1, n_lat):
        block = block + fold_in[d]
    cells = 2 * LANES * (ROWS // BY)

    def spread_blocks(t, to):
        stack = jnp.concatenate(
            [part.astype(F32) for part in parts(block[:, t * AGES:(t + 1) * AGES])], axis=0
        ).astype(jnp.bfloat16)
        widen = jnp.where((iota((96, cells), 0) & 31) == iota((96, cells), 1) >> 5, 1.0, 0.0).astype(jnp.bfloat16)
        planes = lax.dot_general(stack, widen, (((0,), (0,)), ((), ())), preferred_element_type=F32)
        gear_r = jnp.broadcast_to(by_row(gear_v), (AGES, LANES))
        for b in range(cells // LANES):
            to[b] = planes[:, b * LANES:(b + 1) * LANES] * gear_r

    spread_blocks(1, blocks1)
    finish_one()

    spread_blocks(0, blocks)
    interiors(0, 0, AGES - 1)
    last_cohort(0)
    edges(0)
    recruit(0)

    for copy in catch_sends + fold_sends:
        copy.wait_send()
    for t in range(2):
        side, younger, root = month_copies(t)
        one, two = spawn_copies(t)
        for copy in side + one + two:
            copy.wait_send()

        @pl.when(c > 0)
        def _():
            for copy in younger:
                copy.wait_send()

        @pl.when(c == 0)
        def _():
            for copy in root:
                copy.wait_send()

def combine(rest, fix_col, fix_n, fix_s, rec, blocks, consts, fish, grad, out, grad_out, out_v, out_sem):
    ends = [pltpu.make_async_copy(grad, grad_out, out_sem.at[ROWS // BY])]
    ends[0].start()
    for b in range(ROWS // BY):
        rows = slice(b * BY, (b + 1) * BY)
        recruits = [rec[h, rows, :] for h in range(2)]
        catches = [fish[rows, halves(h)] for h in range(2)]

        def step(a, carry):
            made = finished(b, a, rest, fix_col, fix_n, fix_s, blocks, 0, recruits, catches, consts)
            for h in range(2):
                out_v[a, rows, halves(h)] = made[h]
            return carry

        repeat(0, AGES, GROUP, step, 0)
        span = pl.ds(b * BY, BY)
        ends.append(pltpu.make_async_copy(out_v.at[:, span, :], out.at[:, span, :], out_sem.at[b]))
        ends[-1].start()
    for copy in ends:
        copy.wait()


def shards(
    sizes,
    saved, final, prey, heat, sea, fish, offspring,
    death, gear, spread, drift, level, breed,
    landing, east, north, patch, bounds,
):
    n_coh, n_lat, n_lon = sizes
    hbm = pl.BlockSpec(memory_space=pltpu.HBM)
    vmem = pl.BlockSpec(memory_space=pltpu.VMEM)
    given = [
        prey, heat, sea, fish, offspring, spread, drift, level, breed,
        *[v.reshape(1, -1) for v in (gear, spread, drift, level, death, breed)],
        landing, *[v.reshape(1, -1) for v in (east, north, patch)], bounds.T,
    ]
    spaces = [pltpu.VMEM] * 5 + [pltpu.SMEM] * 4 + [pltpu.VMEM] * 11
    plane = (2, ROWS, LANES)
    padded = (AGES + 1, 2, ROWS + PAD, LANES)
    edge_rows, tile, column = (2, 48, LANES), (2, 8, LANES), (ROWS, LANES)
    made = [
        (AGES, *plane), column, (2, AGES, LANES), (2, AGES, LANES), plane,
        (2 * ROWS // BY, AGES, LANES), (3, AGES, LANES), (ROWS, 2 * LANES), (ROWS, 2 * LANES),
    ]

    def f32(shape):
        return pltpu.VMEM(shape, F32)

    scratch = [space(v.shape, v.dtype) for space, v in zip(spaces, given)] + [
        pltpu.VMEM((2, AGES, ROWS, 2 * LANES), jnp.bfloat16),
        pltpu.VMEM((AGES, ROWS, 2 * LANES), jnp.bfloat16),
        f32(padded), f32(padded), f32(made[0]), f32(padded), f32((2, 2, ROWS + PAD, LANES)),
        f32((2, *plane)), f32((2, *plane)), f32(plane), f32(plane), f32(plane), f32(plane),
        *[f32(edge_rows) for _ in range(8)],
        *[f32(tile) for _ in range(4)],
        *[f32(column) for _ in range(10)],
        f32(column), f32(made[2]), f32(made[3]),
        f32(plane), f32(plane), *[f32((2, *plane)) for _ in range(4)],
        f32((32, LANES)), f32((n_lon, SLOTS, LANES)), f32((n_lon, SLOTS, LANES)),
        f32((n_lat, 32, LANES)), f32((n_lat, 32, LANES)),
        f32(made[5]),
        pltpu.SemaphoreType.DMA((3 + GIVEN,)),
        pltpu.SemaphoreType.DMA((52,)),
        pltpu.SemaphoreType.DMA((52,)),
    ]
    states = pl.pallas_call(
        functools.partial(kernel, sizes),
        out_shape=[jax.ShapeDtypeStruct(shape, F32) for shape in made],
        in_specs=[hbm] * (2 + GIVEN),
        out_specs=[vmem] * len(made),
        scratch_shapes=scratch,
        compiler_params=pltpu.CompilerParams(
            collective_id=0, has_side_effects=True, vmem_limit_bytes=32 * 1024 * 1024
        ),
    )(*[pltpu.with_memory_space_constraint(v, pltpu.HBM) for v in (saved, final, *given)])
    return pl.pallas_call(
        combine,
        out_shape=(
            jax.ShapeDtypeStruct((AGES, ROWS, 2 * LANES), F32),
            jax.ShapeDtypeStruct((ROWS, 2 * LANES), F32),
        ),
        in_specs=[vmem] * len(made),
        out_specs=(hbm, hbm),
        scratch_shapes=[f32((AGES, ROWS, 2 * LANES)), pltpu.SemaphoreType.DMA((ROWS // BY + 1,))],
        compiler_params=pltpu.CompilerParams(vmem_limit_bytes=8 * 1024 * 1024),
    )(*states)


def solution(mesh):
    sizes = tuple(mesh.shape[axis] for axis in ("coh", "lat", "lon"))
    tile = P("lat", "lon")
    months = P(None, "lat", "lon")
    rows = ("lat", "lon")
    in_specs = (
        P(None, "coh", "lat", "lon"), P("coh", "lat", "lon"), months, months, tile, tile, tile,
        *[P("coh")] * 6,
        P(rows, None, "coh"), P(rows, None), P(rows), P(rows), P(rows, None),
    )
    out_specs = (P("coh", "lat", "lon"), tile)
    return jax.shard_map(
        functools.partial(shards, sizes), mesh=mesh, in_specs=in_specs, out_specs=out_specs, check_vma=False
    )
```

```python
import functools
import itertools
import jax
import jax.numpy as jnp
from jax import lax
from jax.experimental import pallas as pl
from jax.experimental.pallas import tpu as pltpu
from jax.sharding import PartitionSpec as P

LOG2E = 1.4426950408889634
MESH = pl.DeviceIdType.MESH
F32 = jnp.float32
I32 = jnp.int32

AGES = 32
ROWS = 64
LANES = 128
BY = 16
SLOTS = 4
CODE = 64
PAD = 8
FIRST_AGE = 8
FIELD_LANE = 66
GROUP = 8
GIVEN = 20


def iota(shape, dim):
    return lax.broadcasted_iota(I32, shape, dim)


def as_column(row):
    n = row.shape[1]
    eye = iota((n, n), 0) == iota((n, n), 1)
    return jnp.sum(jnp.where(eye, jnp.broadcast_to(row, (n, n)), 0.0), axis=1, keepdims=True)


def as_row(column):
    n = column.shape[0]
    eye = iota((n, n), 0) == iota((n, n), 1)
    return jnp.sum(jnp.where(eye, jnp.broadcast_to(column, (n, n)), 0.0), axis=0, keepdims=True)


def parts(x):
    high = x.astype(jnp.bfloat16)
    left = x - high.astype(F32)
    mid = left.astype(jnp.bfloat16)
    return high, mid, (left - mid.astype(F32)).astype(jnp.bfloat16)


def selected(onehot, x):
    flags = onehot.astype(jnp.bfloat16)
    return sum(jnp.dot(flags, part, preferred_element_type=F32) for part in parts(x))


def repeat(lo, hi, width, fn, carry):
    def step(n, carry):
        for m in range(width):
            carry = fn(lo + n * width + m, carry)
        return carry

    count = (hi - lo) // width
    if count:
        carry = lax.fori_loop(0, count, step, carry)
    for a in range(lo + count * width, hi):
        carry = fn(a, carry)
    return carry


def halves(h):
    return slice(h * LANES, (h + 1) * LANES)


def finished(b, a, rest, fix_col, fix_n, fix_s, blocks, place, recruits, catches, consts):
    rows = slice(b * BY, (b + 1) * BY)
    lane, row = iota((BY, LANES), 1), iota((BY, LANES), 0)
    turned = fix_col[a, rows, :]
    made = []
    loss, share, scale = (jnp.broadcast_to(consts[n, pl.ds(a, 1), :], (BY, LANES)) for n in range(3))
    for h in range(2):
        moved = rest[a, h, rows, :] - jnp.where(lane == (0, LANES - 1)[h], turned, 0.0)
        for at, end, fix in ((0, 0, fix_n), (ROWS // BY - 1, BY - 1, fix_s)):
            if b == at:
                edge = jnp.broadcast_to(fix[h, pl.ds(a, 1), :], (BY, LANES))
                moved = moved - jnp.where(row == end, edge, 0.0)
        caught = jnp.broadcast_to(blocks[2 * b + h, pl.ds(place + a, 1), :], (BY, LANES))
        survive = jnp.exp2(loss - share * catches[h])
        made.append(survive * moved + recruits[h] * scale + catches[h] * caught)
    return made


def kernel(sizes, saved, final, *refs):
    given, made, scratch = refs[:GIVEN], refs[GIVEN:GIVEN + 9], refs[GIVEN + 9:]
    local, scratch = scratch[:GIVEN], scratch[GIVEN:]
    (
        prey, heat, sea_in, fish, offspring,
        spread, drift, level, breed,
        gear_v, spread_v, drift_v, level_v, death_v, breed_v,
        landing, east, north, patch, bounds,
    ) = local
    (
        saved_v, final_v, adj1, adj0, rest1, hab, hab_e, flow,
        forage, warm, sea, open_e, open_s, rec1,
        row_n1, row_s1, row_n0, row_s0,
        halo_n1, halo_s1, halo_n0, halo_s0,
        diag_n1, diag_s1, diag_n0, diag_s0,
        col1, col0, col_w1, col_e1, col_w0, col_e0,
        dcol_w1, dcol_e1, dcol_w0, dcol_e0,
        fix_col1, fix_n1, fix_s1,
        first1, first0, spawn, spawn_a, spawn_s, spawn_b,
        catch_v, catch_out, catch_in, fold_out, fold_in, blocks1,
        local_sem, send_sem, recv_sem,
    ) = scratch
    rest, fix_col, fix_n, fix_s, rec, blocks, consts, fish_out, grad = made
    n_coh, n_lat, n_lon = sizes
    c, i, j = lax.axis_index("coh"), lax.axis_index("lat"), lax.axis_index("lon")
    c_up, c_dn = lax.rem(c + 1, n_coh), lax.rem(c + n_coh - 1, n_coh)
    i_up, i_dn = lax.rem(i + 1, n_lat), lax.rem(i + n_lat - 1, n_lat)
    j_up, j_dn = lax.rem(j + 1, n_lon), lax.rem(j + n_lon - 1, n_lon)
    total_ages = AGES * n_coh

    def at(cc, ii, jj):
        return {"coh": cc, "lat": ii, "lon": jj}

    load_final = pltpu.make_async_copy(final, final_v, local_sem.at[0])
    load_saved = [pltpu.make_async_copy(saved.at[t], saved_v.at[t], local_sem.at[1 + t]) for t in range(2)]
    fetches = [pltpu.make_async_copy(src, dst, local_sem.at[3 + n]) for n, (src, dst) in enumerate(zip(given, local))]
    aged, others = fetches[8], fetches[3:8] + fetches[9:15]
    for copy in fetches[15:] + [aged, load_saved[1]] + fetches[:3] + [load_final] + others + [load_saved[0]]:
        copy.start()

    barrier = pltpu.get_barrier_semaphore()
    partners = [at(c, i, lax.rem(j + d, n_lon)) for d in range(1, n_lon)]
    partners += [at(c, lax.rem(i + d, n_lat), j) for d in range(1, n_lat)]
    partners += [at(lax.rem(c + d, n_coh), i, j) for d in range(1, n_coh)]
    partners += [at(cc, ii, j) for cc in (c_up, c_dn) for ii in (i_up, i_dn)]
    partners += [at(cc, i, jj) for cc in (c_up, c_dn) for jj in (j_up, j_dn)]
    for partner in partners:
        pl.semaphore_signal(barrier, inc=1, device_id=partner, device_id_type=MESH)

    def remote(src, dst, k, to):
        return pltpu.make_async_remote_copy(
            src_ref=src, dst_ref=dst, send_sem=send_sem.at[k], recv_sem=recv_sem.at[k],
            device_id=to, device_id_type=MESH,
        )

    lane = iota((BY, LANES), 1)
    lane_all = iota((ROWS, LANES), 1)
    even_all = (lane_all & 1) == 0

    def mature(a):
        return (c * AGES + a + 1).astype(F32) * (1.0 / total_ages) * breed[a]

    for copy in fetches[15:]:
        copy.wait()
    east_row = east[...].astype(F32)
    east_col = as_column(east_row)
    same = jnp.broadcast_to(east_col, (32, 32)) == jnp.broadcast_to(east_row, (32, 32))
    ahead = same & (iota((32, 32), 0) < iota((32, 32), 1))
    rank_row = jnp.sum(jnp.where(ahead, 1.0, 0.0), axis=0, keepdims=True)
    slot_row = east_row * SLOTS + rank_row
    code_col = as_column((north[...] * 32 + patch[...]).astype(F32))
    cohort = (c * AGES + iota((32, AGES), 1)).astype(F32)
    lower, upper = (as_column(bounds[n:n + 1, :].astype(F32)) for n in range(2))
    inside = (cohort >= lower) & (cohort < upper)
    catch_v[...] = jnp.broadcast_to(code_col, (32, LANES))
    catch_v[:, 0:32] = jnp.where(inside, landing[:, 0, :], 0.0)
    catch_v[:, 32:64] = jnp.where(inside, landing[:, 1, :], 0.0)
    slots = n_lon * SLOTS
    place = jnp.where(iota((slots, 32), 0).astype(F32) == jnp.broadcast_to(slot_row, (slots, 32)), 1.0, 0.0)
    catch_out[...] = selected(place, catch_v[...]).reshape(n_lon, SLOTS, LANES)
    catch_in[j] = catch_out[j]

    pl.semaphore_wait(barrier, len(partners))

    catch_sends = [
        remote(catch_out.at[lax.rem(j + d, n_lon)], catch_in.at[j], d, at(c, i, lax.rem(j + d, n_lon)))
        for d in range(1, n_lon)
    ]
    for copy in catch_sends:
        copy.start()

    k_fold, k_spawn, k_month = 16, 20, 28

    pair = (c + 1 - 2 * lax.rem(c, 2), n_coh - 1 - c)

    def spawn_copies(t):
        one = [remote(spawn.at[t, h], spawn_a.at[t, h], k_spawn + 2 * t + h, at(pair[h], i, j)) for h in range(2)]
        two = [
            remote(spawn_s.at[t, h], spawn_b.at[t, h], k_spawn + 4 + 2 * t + h, at(pair[1 - h], i, j)) for h in range(2)
        ]
        return one, two

    def spawn_part(t):
        def add(a, total):
            return total + mature(a) * saved_v[t, a].astype(F32)

        load_saved[t].wait()
        total = repeat(0, AGES, 8, add, jnp.zeros((ROWS, 2 * LANES), F32))
        for h in range(2):
            spawn[t, h] = total[:, halves(h)]
        for copy in spawn_copies(t)[0]:
            copy.start()

    def spawn_turn(t):
        one, two = spawn_copies(t)
        for h in range(2):
            one[h].wait_recv()
            spawn_s[t, h] = spawn[t, h] + spawn_a[t, h]
            two[h].start()

    aged.wait()
    spawn_part(1)

    body = slice(0, ROWS)
    for copy in fetches[:3]:
        copy.wait()
    for h in range(2):
        sea[h] = sea_in[:, halves(h)].astype(F32)
    last_lane = lane_all == LANES - 1
    sea0, sea1 = sea[0], sea[1]
    turned1 = pltpu.roll(sea1, LANES - 1, 1)
    open_e[0] = sea0 * jnp.where(last_lane, turned1, pltpu.roll(sea0, LANES - 1, 1))
    open_e[1] = sea1 * jnp.where(last_lane, 0.0, turned1)
    last_row = iota((ROWS, LANES), 0) == ROWS - 1
    pad = jnp.zeros((PAD, LANES), F32)
    for h, here in enumerate((sea0, sea1)):
        open_s[h] = here * jnp.where(last_row, 0.0, pltpu.roll(here, ROWS - 1, 0))
        flow[0, h, 0:PAD, :] = pad
        flow[1, h, 0:PAD, :] = pad
        for t in range(2):
            forage[t, h] = here * prey[t, :, halves(h)]
            warm[t, h] = heat[t, :, halves(h)] * 0.25

    def field(f, h):
        if f == 4:
            return sea[h]
        return (forage, warm)[f % 2][1 - f // 2, h]

    columns = jnp.zeros((ROWS, LANES), F32)
    for h in range(2):
        row_n1[h, 0:8, :] = pad
        row_s1[h, 0:8, :] = pad
    for f in range(5):
        for h in range(2):
            plane = field(f, h)
            row_n1[h, f:f + 1, :] = plane[0:1]
            row_s1[h, f:f + 1, :] = plane[ROWS - 1:ROWS]
        columns = jnp.where(lane_all == FIELD_LANE + 2 * f, jnp.broadcast_to(field(f, 0)[:, 0:1], (ROWS, LANES)), columns)
        columns = jnp.where(
            lane_all == FIELD_LANE + 2 * f + 1, jnp.broadcast_to(field(f, 1)[:, LANES - 1:], (ROWS, LANES)), columns
        )

    def clear_pads(ref, a):
        for h in range(2):
            ref[a, h, ROWS:, :] = pad

    def pick_columns(a, x0, x1):
        width = iota(x0.shape, 1)
        edges = jnp.where(width == 0, x0, x1)
        return ((width + 1) & 127) >> 1 == a, pltpu.roll(edges, 2 * a, 1)

    def eastward(x0, x1):
        turned1 = pltpu.roll(x1, LANES - 1, 1)
        edge = iota(x0.shape, 1) == LANES - 1
        return jnp.where(edge, turned1, pltpu.roll(x0, LANES - 1, 1)), turned1

    load_final.wait()

    def unpack(a, columns):
        x = final_v[a].astype(F32)
        x0, x1 = x[:, :LANES], x[:, LANES:]
        clear_pads(adj1, a)
        clear_pads(adj0, a)
        for h, xh in enumerate((x0, x1)):
            adj1[a, h, body, :] = xh
            row_n1[h, pl.ds(FIRST_AGE + a, 1), :] = xh[0:1]
            row_s1[h, pl.ds(FIRST_AGE + a, 1), :] = xh[ROWS - 1:]
        mine, moved = pick_columns(a, x0, x1)
        return jnp.where(mine, moved, columns)

    col1[...] = repeat(0, AGES, 8, unpack, columns)
    clear_pads(adj1, AGES)
    clear_pads(adj0, AGES)

    def month_copies(t):
        k = k_month + 12 * (1 - t)
        adj = (adj0, adj1)[t]
        col = (col0, col1)[t]
        span = slice(0, 40) if t == 1 else slice(FIRST_AGE, 40)
        row_n, row_s = ((row_n0, row_s0), (row_n1, row_s1))[t]
        halo_n, halo_s = ((halo_n0, halo_s0), (halo_n1, halo_s1))[t]
        diag_n, diag_s = ((diag_n0, diag_s0), (diag_n1, diag_s1))[t]
        col_w, col_e = ((col_w0, col_e0), (col_w1, col_e1))[t]
        dcol_w, dcol_e = ((dcol_w0, dcol_e0), (dcol_w1, dcol_e1))[t]
        first = (first0, first1)[t]
        side = [
            remote(row_n.at[:, span, :], halo_s.at[:, span, :], k, at(c, i_dn, j)),
            remote(row_s.at[:, span, :], halo_n.at[:, span, :], k + 1, at(c, i_up, j)),
            remote(col, col_e, k + 4, at(c, i, j_dn)),
            remote(col, col_w, k + 5, at(c, i, j_up)),
        ]
        younger = [
            remote(adj.at[0, :, body, :], adj.at[AGES, :, body, :], k + 8, at(c_dn, i, j)),
            remote(adj.at[0, :, 0:8, :], diag_s, k + 2, at(c_dn, i_dn, j)),
            remote(adj.at[0, :, ROWS - 8:ROWS, :], diag_n, k + 3, at(c_dn, i_up, j)),
            remote(col, dcol_e, k + 6, at(c_dn, i, j_dn)),
            remote(col, dcol_w, k + 7, at(c_dn, i, j_up)),
        ]
        root = [remote(adj.at[0, :, body, :], first, k + 8 + d, at(d, i, j)) for d in range(1, n_coh)]
        return side, younger, root

    def start_planes(t):
        side, younger, root = month_copies(t)
        adj, first = (adj0, adj1)[t], (first0, first1)[t]

        @pl.when(c > 0)
        def _():
            for copy in younger[:3]:
                copy.start()

        @pl.when(c == 0)
        def _():
            for copy in root:
                copy.start()
            for h in range(2):
                first[h] = adj[0, h, body, :]

    def start_edges(t):
        side, younger, root = month_copies(t)
        for copy in side:
            copy.start()

        @pl.when(c > 0)
        def _():
            for copy in younger[3:]:
                copy.start()

    start_planes(1)
    start_edges(1)

    for copy in others:
        copy.wait()
    spawn_part(0)
    fish_out[...] = fish[...]
    seniority = (c * AGES + iota((AGES, LANES), 0) + 1).astype(F32) * (1.0 / total_ages)
    consts[0] = jnp.broadcast_to(as_column(death_v[...]) * -LOG2E, (AGES, LANES))
    consts[1] = jnp.broadcast_to(as_column(gear_v[...]) * LOG2E, (AGES, LANES))
    consts[2] = jnp.broadcast_to(as_column(breed_v[...]), (AGES, LANES)) * seniority

    def habitats(t):
        def step(a, carry):
            drift_a, level_a = drift[a], level[a] * 0.25
            for r in range(0, ROWS, BY):
                rows = slice(r, r + BY)
                found = []
                for h in range(2):
                    q = warm[t, h, rows, :] - level_a
                    found.append(forage[t, h, rows, :] * drift_a / (1.0 + q * q))
                    hab[a, h, rows, :] = found[h]
                if t == 0:
                    for h, ahead in enumerate(eastward(*found)):
                        hab_e[a, h, rows, :] = ahead
            if t == 1:
                clear_pads(hab, a)
            return carry

        repeat(0, AGES, 4, step, 0)

    def interior(t, adj, into, a, flow):
        spread_a = spread[a]
        for r in range(0, ROWS, BY):
            mid, dn = slice(r, r + BY), slice(r + 1, r + 1 + BY)
            h0, h1 = hab[a, 0, mid, :], hab[a, 1, mid, :]
            l0, l1 = adj[a + 1, 0, mid, :], adj[a + 1, 1, mid, :]
            lr0, lr1 = eastward(l0, l1)
            hr0, hr1 = eastward(h0, h1) if t == 1 else (hab_e[a, 0, mid, :], hab_e[a, 1, mid, :])
            kept, given = [], []
            for h, hh, ll, hr, lr in ((0, h0, l0, hr0, lr0), (1, h1, l1, hr1, lr1)):
                g = hr - hh
                k = jnp.maximum(g, 0.0) + spread_a
                o = open_e[h, mid, :] * (ll - lr)
                y = ll - k * o
                given.append((k - g) * o)
                g = hab[a, h, dn, :] - hh
                k = jnp.maximum(g, 0.0) + spread_a
                o = open_s[h, mid, :] * (ll - adj[a + 1, h, dn, :])
                flow[h, dn, :] = (k - g) * o
                kept.append(y - k * o)
            m0, m1 = pltpu.roll(given[0], 1, 1), pltpu.roll(given[1], 1, 1)
            into[a, 0, mid, :] = kept[0] + (flow[0, mid, :] + jnp.where(lane == 0, m1, m0))
            into[a, 1, mid, :] = kept[1] + (flow[1, mid, :] + jnp.where(lane == 0, m0, m1))

    def interiors(t, lo, hi):
        adj, into = (adj0, adj1)[t], (rest, rest1)[t]
        turns = itertools.count()

        def step(a, carry):
            interior(t, adj, into, a, flow.at[next(turns) % 2])
            return carry

        repeat(lo, hi, 2, step, 0)

    age_of = iota((AGES, LANES), 0)
    lane_age = ((iota((AGES, LANES), 1) + 1) & 127) >> 1

    def by_row(v):
        return as_column(v[...])

    def by_lane(v):
        wide = jnp.broadcast_to(by_row(v), (AGES, LANES))
        return jnp.sum(jnp.where(age_of == lane_age, wide, 0.0), axis=0, keepdims=True)

    north_open = jnp.where(i > 0, 1.0, 0.0)
    south_open = jnp.where(i < n_lat - 1, 1.0, 0.0)
    west_open = jnp.where(j > 0, 1.0, 0.0)
    east_open = jnp.where(j < n_lon - 1, 1.0, 0.0)

    def edges(t):
        adj = (adj0, adj1)[t]
        side, younger, root = month_copies(t)
        halo_n, halo_s = ((halo_n0, halo_s0), (halo_n1, halo_s1))[t]
        row_n, row_s = ((row_n0, row_s0), (row_n1, row_s1))[t]
        diag_n, diag_s = ((diag_n0, diag_s0), (diag_n1, diag_s1))[t]
        col = (col0, col1)[t]
        col_w, col_e = ((col_w0, col_e0), (col_w1, col_e1))[t]
        dcol_w, dcol_e = ((dcol_w0, dcol_e0), (dcol_w1, dcol_e1))[t]
        for copy in side:
            copy.wait_recv()

        @pl.when(c < n_coh - 1)
        def _():
            for copy in younger[1:]:
                copy.wait_recv()

        @pl.when(c == n_coh - 1)
        def _():
            diag_n[...] = jnp.zeros_like(diag_n)
            diag_s[...] = jnp.zeros_like(diag_s)
            dcol_w[...] = jnp.zeros_like(dcol_w)
            dcol_e[...] = jnp.zeros_like(dcol_e)

        past = FIRST_AGE + AGES
        for h in range(2):
            row_n[h, past:past + 1, :] = adj[AGES, h, 0:1, :]
            row_s[h, past:past + 1, :] = adj[AGES, h, ROWS - 1:ROWS, :]
            halo_n[h, past:past + 1, :] = diag_n[h, 7:8, :]
            halo_s[h, past:past + 1, :] = diag_s[h, 0:1, :]
        later = slice(FIRST_AGE + 1, FIRST_AGE + 1 + AGES)
        f = 2 * (1 - t)
        to_col, to_n, to_s = ((fix_col, fix_n, fix_s), (fix_col1, fix_n1, fix_s1))[t]
        spread_r, drift_r, level_r = (
            jnp.broadcast_to(x, (AGES, LANES)) for x in (by_row(spread_v), by_row(drift_v), by_row(level_v) * 0.25)
        )
        for own, halo, own1, halo1, gate, fix in (
            (row_n, halo_n, row_n1, halo_n1, north_open, to_n),
            (row_s, halo_s, row_s1, halo_s1, south_open, to_s),
        ):
            for h in range(2):
                def habitat(buf):
                    q = buf[h, f + 1:f + 2, :] - level_r
                    return buf[h, f:f + 1, :] * drift_r / (1.0 + q * q)

                passage = own1[h, 4:5, :] * halo1[h, 4:5, :] * gate
                k = spread_r + jnp.maximum(habitat(halo1) - habitat(own1), 0.0)
                fix[h] = passage * k * (own[h, later, :] - halo[h, later, :])

        def both(own_w, own_e):
            wide = (ROWS, LANES)
            return jnp.where(even_all, jnp.broadcast_to(own_w, wide), jnp.broadcast_to(own_e, wide))

        def own_field(f):
            return both(field(f, 0)[:, 0:1], field(f, 1)[:, LANES - 1:])

        def halo_field(f):
            spot = FIELD_LANE + 2 * f
            return both(col_w1[:, spot + 1:spot + 2], col_e1[:, spot:spot + 1])

        spread_l, drift_l, level_l = (by_lane(x) for x in (spread_v, drift_v, level_v))

        def habitat_columns(get):
            q = get(f + 1) - level_l * 0.25
            return get(f) * drift_l / (1.0 + q * q)

        passage = own_field(4) * halo_field(4) * jnp.where(even_all, west_open, east_open)
        mine, moved = pick_columns(AGES, adj[AGES, 0, body, :], adj[AGES, 1, body, :])
        own = pltpu.roll(jnp.where(mine, moved, col[...]), LANES - 2, 1)
        other = jnp.where(even_all, pltpu.roll(col_w[...], LANES - 1, 1), pltpu.roll(col_e[...], LANES - 3, 1))
        other = jnp.where(lane_all == 62, pltpu.roll(dcol_w[...], 63, 1), other)
        other = jnp.where(lane_all == 61, pltpu.roll(dcol_e[...], 61, 1), other)
        k = spread_l + jnp.maximum(habitat_columns(halo_field) - habitat_columns(own_field), 0.0)
        fix = passage * k * (own - other)
        for a in range(AGES):
            to_col[a] = pltpu.roll(fix, (LANES - 2 * a) % LANES, 1)

    def finish_one():
        def put(b, a, columns, recruits, catches):
            made = finished(b, a, rest1, fix_col1, fix_n1, fix_s1, blocks1, 0, recruits, catches, consts)
            for h in range(2):
                adj0[a, h, b * BY:(b + 1) * BY, :] = made[h]
                if b == 0:
                    row_n0[h, pl.ds(FIRST_AGE + a, 1), :] = made[h][0:1]
                if b == ROWS // BY - 1:
                    row_s0[h, pl.ds(FIRST_AGE + a, 1), :] = made[h][BY - 1:]
            mine, moved = pick_columns(a, made[0], made[1])
            return jnp.where(mine, moved, columns)

        def block(b):
            rows = slice(b * BY, (b + 1) * BY)
            return rows, [rec1[h, rows, :] for h in range(2)], [fish[rows, halves(h)] for h in range(2)]

        for b in range(ROWS // BY):
            rows, recruits, catches = block(b)
            col0[rows, :] = put(b, 0, jnp.zeros((BY, LANES), F32), recruits, catches)
        start_planes(0)
        for b in range(ROWS // BY):
            rows, recruits, catches = block(b)

            def step(group, columns):
                for n in range(GROUP):
                    columns = put(b, group * GROUP + n, columns, recruits, catches)
                return columns

            columns = col0[rows, :]
            for a in range(1, GROUP):
                columns = put(b, a, columns, recruits, catches)
            col0[rows, :] = lax.fori_loop(1, AGES // GROUP, step, columns)
        start_edges(0)

    def last_cohort(t):
        adj = (adj0, adj1)[t]
        side, younger, root = month_copies(t)

        @pl.when(c < n_coh - 1)
        def _():
            younger[0].wait_recv()

        @pl.when(c == n_coh - 1)
        def _():
            for h in range(2):
                adj[AGES, h, body, :] = jnp.zeros((ROWS, LANES), F32)

        interiors(t, AGES - 1, AGES)

    def recruit(t):
        first = (first0, first1)[t]
        side, younger, root = month_copies(t)
        for d in range(1, n_coh):
            @pl.when(c == d)
            def _():
                root[d - 1].wait_recv()
        two = spawn_copies(t)[1]
        for h in range(2):
            two[h].wait_recv()
            total = spawn_s[t, h] + spawn_b[t, h]
            ratio = 1.0 / (1.0 + total)
            base = first[h] * sea[h]
            (rec, rec1)[t][h] = base * offspring[:, halves(h)] * ratio * ratio
            gain = base * total * ratio
            if t == 1:
                grad[:, halves(h)] = gain
            else:
                grad[:, halves(h)] = grad[:, halves(h)] + gain

    fold_sends = [
        remote(fold_out.at[lax.rem(i + d, n_lat)], fold_in.at[i], k_fold + d, at(c, lax.rem(i + d, n_lat), j))
        for d in range(1, n_lat)
    ]

    habitats(1)
    spawn_turn(1)
    interiors(1, 0, 14)
    for copy in catch_sends:
        copy.wait_recv()
    got = catch_in[...].reshape(slots, LANES)
    half = n_lat * 16
    code_row = as_row(got[:, CODE:CODE + 1])
    wanted = iota((2 * half, slots), 0)
    low = wanted & (half - 1)
    code = ((low >> 4) * 32 + (low & 15) + jnp.where(wanted < half, 0, 16)).astype(F32)
    pick = jnp.where(code == jnp.broadcast_to(code_row, (2 * half, slots)), 1.0, 0.0)
    folded = selected(pick, got)
    packed = jnp.where(iota((half, LANES), 1) < 64, folded[:half], pltpu.roll(folded[half:], 64, 1))
    fold_out[...] = packed.reshape(n_lat, 16, LANES)
    fold_in[i] = fold_out[i]
    for copy in fold_sends:
        copy.start()
    interiors(1, 14, AGES - 1)
    last_cohort(1)
    habitats(0)
    edges(1)
    spawn_turn(0)
    recruit(1)
    for copy in fold_sends:
        copy.wait_recv()
    block = fold_in[0]
    for d in range(1, n_lat):
        block = block + fold_in[d]
    block = jnp.concatenate([block, pltpu.roll(block, 64, 1)], axis=0)
    cells = 2 * LANES * (ROWS // BY)

    def spread_blocks(t, to):
        stack = jnp.concatenate(
            [part.astype(F32) for part in parts(block[:, t * AGES:(t + 1) * AGES])], axis=0
        ).astype(jnp.bfloat16)
        widen = jnp.where((iota((96, cells), 0) & 31) == iota((96, cells), 1) >> 5, 1.0, 0.0).astype(jnp.bfloat16)
        planes = lax.dot_general(stack, widen, (((0,), (0,)), ((), ())), preferred_element_type=F32)
        gear_r = jnp.broadcast_to(by_row(gear_v), (AGES, LANES))
        for b in range(cells // LANES):
            to[b] = planes[:, b * LANES:(b + 1) * LANES] * gear_r

    spread_blocks(1, blocks1)
    finish_one()

    interiors(0, 0, AGES - 1)
    spread_blocks(0, blocks)
    last_cohort(0)
    edges(0)
    recruit(0)

    for copy in catch_sends + fold_sends:
        copy.wait_send()
    for t in range(2):
        side, younger, root = month_copies(t)
        one, two = spawn_copies(t)
        for copy in side + one + two:
            copy.wait_send()

        @pl.when(c > 0)
        def _():
            for copy in younger:
                copy.wait_send()

        @pl.when(c == 0)
        def _():
            for copy in root:
                copy.wait_send()

def combine(rest, fix_col, fix_n, fix_s, rec, blocks, consts, fish, grad, out, grad_out, out_v, out_sem):
    ends = [pltpu.make_async_copy(grad, grad_out, out_sem.at[ROWS // BY])]
    ends[0].start()
    for b in range(ROWS // BY):
        rows = slice(b * BY, (b + 1) * BY)
        recruits = [rec[h, rows, :] for h in range(2)]
        catches = [fish[rows, halves(h)] for h in range(2)]

        def step(a, carry):
            made = finished(b, a, rest, fix_col, fix_n, fix_s, blocks, 0, recruits, catches, consts)
            for h in range(2):
                out_v[a, rows, halves(h)] = made[h]
            return carry

        repeat(0, AGES, GROUP, step, 0)
        span = pl.ds(b * BY, BY)
        ends.append(pltpu.make_async_copy(out_v.at[:, span, :], out.at[:, span, :], out_sem.at[b]))
        ends[-1].start()
    for copy in ends:
        copy.wait()


def shards(
    sizes,
    saved, final, prey, heat, sea, fish, offspring,
    death, gear, spread, drift, level, breed,
    landing, east, north, patch, bounds,
):
    n_coh, n_lat, n_lon = sizes
    hbm = pl.BlockSpec(memory_space=pltpu.HBM)
    vmem = pl.BlockSpec(memory_space=pltpu.VMEM)
    given = [
        prey, heat, sea, fish, offspring, spread, drift, level, breed,
        *[v.reshape(1, -1) for v in (gear, spread, drift, level, death, breed)],
        landing, *[v.reshape(1, -1) for v in (east, north, patch)], bounds.T,
    ]
    spaces = [pltpu.VMEM] * 5 + [pltpu.SMEM] * 4 + [pltpu.VMEM] * 11
    plane = (2, ROWS, LANES)
    padded = (AGES + 1, 2, ROWS + PAD, LANES)
    edge_rows, tile, column = (2, 48, LANES), (2, 8, LANES), (ROWS, LANES)
    made = [
        (AGES, *plane), (AGES, *column), (2, AGES, LANES), (2, AGES, LANES), plane,
        (2 * ROWS // BY, AGES, LANES), (3, AGES, LANES), (ROWS, 2 * LANES), (ROWS, 2 * LANES),
    ]

    def f32(shape):
        return pltpu.VMEM(shape, F32)

    scratch = [space(v.shape, v.dtype) for space, v in zip(spaces, given)] + [
        pltpu.VMEM((2, AGES, ROWS, 2 * LANES), jnp.bfloat16),
        pltpu.VMEM((AGES, ROWS, 2 * LANES), jnp.bfloat16),
        f32(padded), f32(padded), f32(made[0]), f32(padded), f32(made[0]), f32((2, 2, ROWS + PAD, LANES)),
        f32((2, *plane)), f32((2, *plane)), f32(plane), f32(plane), f32(plane), f32(plane),
        *[f32(edge_rows) for _ in range(8)],
        *[f32(tile) for _ in range(4)],
        *[f32(column) for _ in range(10)],
        f32(made[1]), f32(made[2]), f32(made[3]),
        f32(plane), f32(plane), *[f32((2, *plane)) for _ in range(4)],
        f32((32, LANES)), f32((n_lon, SLOTS, LANES)), f32((n_lon, SLOTS, LANES)),
        f32((n_lat, 16, LANES)), f32((n_lat, 16, LANES)),
        f32(made[5]),
        pltpu.SemaphoreType.DMA((3 + GIVEN,)),
        pltpu.SemaphoreType.DMA((52,)),
        pltpu.SemaphoreType.DMA((52,)),
    ]
    states = pl.pallas_call(
        functools.partial(kernel, sizes),
        out_shape=[jax.ShapeDtypeStruct(shape, F32) for shape in made],
        in_specs=[hbm] * (2 + GIVEN),
        out_specs=[vmem] * len(made),
        scratch_shapes=scratch,
        compiler_params=pltpu.CompilerParams(
            collective_id=0, has_side_effects=True, vmem_limit_bytes=32 * 1024 * 1024
        ),
    )(*[pltpu.with_memory_space_constraint(v, pltpu.HBM) for v in (saved, final, *given)])
    return pl.pallas_call(
        combine,
        out_shape=(
            jax.ShapeDtypeStruct((AGES, ROWS, 2 * LANES), F32),
            jax.ShapeDtypeStruct((ROWS, 2 * LANES), F32),
        ),
        in_specs=[vmem] * len(made),
        out_specs=(hbm, hbm),
        scratch_shapes=[f32((AGES, ROWS, 2 * LANES)), pltpu.SemaphoreType.DMA((ROWS // BY + 1,))],
        compiler_params=pltpu.CompilerParams(vmem_limit_bytes=8 * 1024 * 1024),
    )(*states)


def solution(mesh):
    sizes = tuple(mesh.shape[axis] for axis in ("coh", "lat", "lon"))
    tile = P("lat", "lon")
    months = P(None, "lat", "lon")
    rows = ("lat", "lon")
    in_specs = (
        P(None, "coh", "lat", "lon"), P("coh", "lat", "lon"), months, months, tile, tile, tile,
        *[P("coh")] * 6,
        P(rows, None, "coh"), P(rows, None), P(rows), P(rows), P(rows, None),
    )
    out_specs = (P("coh", "lat", "lon"), tile)
    return jax.shard_map(
        functools.partial(shards, sizes), mesh=mesh, in_specs=in_specs, out_specs=out_specs, check_vma=False
    )
```

```python
import functools
import itertools
import jax
import jax.numpy as jnp
from jax import lax
from jax.experimental import pallas as pl
from jax.experimental.pallas import tpu as pltpu
from jax.sharding import PartitionSpec as P

LOG2E = 1.4426950408889634
MESH = pl.DeviceIdType.MESH
F32 = jnp.float32
I32 = jnp.int32

AGES = 32
ROWS = 64
LANES = 128
BY = 16
SLOTS = 4
CODE = 64
PAD = 8
FIRST_AGE = 8
FIELD_LANE = 66
GROUP = 8
GIVEN = 20


def iota(shape, dim):
    return lax.broadcasted_iota(I32, shape, dim)


def as_column(row):
    n = row.shape[1]
    eye = iota((n, n), 0) == iota((n, n), 1)
    return jnp.sum(jnp.where(eye, jnp.broadcast_to(row, (n, n)), 0.0), axis=1, keepdims=True)


def as_row(column):
    n = column.shape[0]
    eye = iota((n, n), 0) == iota((n, n), 1)
    return jnp.sum(jnp.where(eye, jnp.broadcast_to(column, (n, n)), 0.0), axis=0, keepdims=True)


def parts(x):
    high = x.astype(jnp.bfloat16)
    left = x - high.astype(F32)
    mid = left.astype(jnp.bfloat16)
    return high, mid, (left - mid.astype(F32)).astype(jnp.bfloat16)


def selected(onehot, x):
    flags = onehot.astype(jnp.bfloat16)
    return sum(jnp.dot(flags, part, preferred_element_type=F32) for part in parts(x))


def repeat(lo, hi, width, fn, carry):
    def step(n, carry):
        for m in range(width):
            carry = fn(lo + n * width + m, carry)
        return carry

    count = (hi - lo) // width
    if count:
        carry = lax.fori_loop(0, count, step, carry)
    for a in range(lo + count * width, hi):
        carry = fn(a, carry)
    return carry


def halves(h):
    return slice(h * LANES, (h + 1) * LANES)


def finished(b, a, rest, fix_col, fix_n, fix_s, blocks, place, recruits, catches, consts):
    rows = slice(b * BY, (b + 1) * BY)
    lane, row = iota((BY, LANES), 1), iota((BY, LANES), 0)
    turned = fix_col[a, rows, :]
    made = []
    loss, share, scale = (jnp.broadcast_to(consts[n, pl.ds(a, 1), :], (BY, LANES)) for n in range(3))
    for h in range(2):
        moved = rest[a, h, rows, :] - jnp.where(lane == (0, LANES - 1)[h], turned, 0.0)
        for at, end, fix in ((0, 0, fix_n), (ROWS // BY - 1, BY - 1, fix_s)):
            if b == at:
                edge = jnp.broadcast_to(fix[h, pl.ds(a, 1), :], (BY, LANES))
                moved = moved - jnp.where(row == end, edge, 0.0)
        caught = jnp.broadcast_to(blocks[2 * b + h, pl.ds(place + a, 1), :], (BY, LANES))
        survive = jnp.exp2(loss - share * catches[h])
        made.append(survive * moved + recruits[h] * scale + catches[h] * caught)
    return made


def kernel(sizes, saved, final, *refs):
    given, made, scratch = refs[:GIVEN], refs[GIVEN:GIVEN + 9], refs[GIVEN + 9:]
    local, scratch = scratch[:GIVEN], scratch[GIVEN:]
    (
        prey, heat, sea_in, fish, offspring,
        spread, drift, level, breed,
        gear_v, spread_v, drift_v, level_v, death_v, breed_v,
        landing, east, north, patch, bounds,
    ) = local
    (
        saved_v, final_v, adj1, adj0, rest1, hab, hab_e, flow,
        forage, warm, sea, open_e, open_s, rec1,
        row_n1, row_s1, row_n0, row_s0,
        halo_n1, halo_s1, halo_n0, halo_s0,
        diag_n1, diag_s1, diag_n0, diag_s0,
        col1, col0, col_w1, col_e1, col_w0, col_e0,
        dcol_w1, dcol_e1, dcol_w0, dcol_e0,
        fix_col1, fix_n1, fix_s1,
        first1, first0, spawn, spawn_a, spawn_s, spawn_b,
        catch_v, catch_out, catch_in, fold_out, fold_in, blocks1,
        local_sem, send_sem, recv_sem,
    ) = scratch
    rest, fix_col, fix_n, fix_s, rec, blocks, consts, fish_out, grad = made
    n_coh, n_lat, n_lon = sizes
    c, i, j = lax.axis_index("coh"), lax.axis_index("lat"), lax.axis_index("lon")
    c_up, c_dn = lax.rem(c + 1, n_coh), lax.rem(c + n_coh - 1, n_coh)
    i_up, i_dn = lax.rem(i + 1, n_lat), lax.rem(i + n_lat - 1, n_lat)
    j_up, j_dn = lax.rem(j + 1, n_lon), lax.rem(j + n_lon - 1, n_lon)
    total_ages = AGES * n_coh

    def at(cc, ii, jj):
        return {"coh": cc, "lat": ii, "lon": jj}

    load_final = pltpu.make_async_copy(final, final_v, local_sem.at[0])
    load_saved = [pltpu.make_async_copy(saved.at[t], saved_v.at[t], local_sem.at[1 + t]) for t in range(2)]
    fetches = [pltpu.make_async_copy(src, dst, local_sem.at[3 + n]) for n, (src, dst) in enumerate(zip(given, local))]
    aged, others = fetches[8], fetches[3:8] + fetches[9:15]
    for copy in fetches[15:] + [aged, load_saved[1]] + fetches[:3] + [load_final] + others + [load_saved[0]]:
        copy.start()

    barrier = pltpu.get_barrier_semaphore()
    partners = [at(c, i, lax.rem(j + d, n_lon)) for d in range(1, n_lon)]
    partners += [at(c, lax.rem(i + d, n_lat), j) for d in range(1, n_lat)]
    partners += [at(lax.rem(c + d, n_coh), i, j) for d in range(1, n_coh)]
    partners += [at(cc, ii, j) for cc in (c_up, c_dn) for ii in (i_up, i_dn)]
    partners += [at(cc, i, jj) for cc in (c_up, c_dn) for jj in (j_up, j_dn)]
    for partner in partners:
        pl.semaphore_signal(barrier, inc=1, device_id=partner, device_id_type=MESH)

    def remote(src, dst, k, to):
        return pltpu.make_async_remote_copy(
            src_ref=src, dst_ref=dst, send_sem=send_sem.at[k], recv_sem=recv_sem.at[k],
            device_id=to, device_id_type=MESH,
        )

    lane = iota((BY, LANES), 1)
    lane_all = iota((ROWS, LANES), 1)
    even_all = (lane_all & 1) == 0

    def mature(a):
        return (c * AGES + a + 1).astype(F32) * (1.0 / total_ages) * breed[a]

    for copy in fetches[15:]:
        copy.wait()
    east_row = east[...].astype(F32)
    east_col = as_column(east_row)
    same = jnp.broadcast_to(east_col, (32, 32)) == jnp.broadcast_to(east_row, (32, 32))
    ahead = same & (iota((32, 32), 0) < iota((32, 32), 1))
    rank_row = jnp.sum(jnp.where(ahead, 1.0, 0.0), axis=0, keepdims=True)
    slot_row = east_row * SLOTS + rank_row
    code_col = as_column((north[...] * 32 + patch[...]).astype(F32))
    cohort = (c * AGES + iota((32, AGES), 1)).astype(F32)
    lower, upper = (as_column(bounds[n:n + 1, :].astype(F32)) for n in range(2))
    inside = (cohort >= lower) & (cohort < upper)
    catch_v[...] = jnp.broadcast_to(code_col, (32, LANES))
    catch_v[:, 0:32] = jnp.where(inside, landing[:, 0, :], 0.0)
    catch_v[:, 32:64] = jnp.where(inside, landing[:, 1, :], 0.0)
    slots = n_lon * SLOTS
    place = jnp.where(iota((slots, 32), 0).astype(F32) == jnp.broadcast_to(slot_row, (slots, 32)), 1.0, 0.0)
    catch_out[...] = selected(place, catch_v[...]).reshape(n_lon, SLOTS, LANES)
    catch_in[j] = catch_out[j]

    pl.semaphore_wait(barrier, len(partners))

    catch_sends = [
        remote(catch_out.at[lax.rem(j + d, n_lon)], catch_in.at[j], d, at(c, i, lax.rem(j + d, n_lon)))
        for d in range(1, n_lon)
    ]
    for copy in catch_sends:
        copy.start()

    k_fold, k_spawn, k_month = 16, 20, 28

    pair = (c + 1 - 2 * lax.rem(c, 2), n_coh - 1 - c)

    def spawn_copies(t):
        one = [remote(spawn.at[t, h], spawn_a.at[t, h], k_spawn + 2 * t + h, at(pair[h], i, j)) for h in range(2)]
        two = [
            remote(spawn_s.at[t, h], spawn_b.at[t, h], k_spawn + 4 + 2 * t + h, at(pair[1 - h], i, j)) for h in range(2)
        ]
        return one, two

    def spawn_part(t):
        def add(a, total):
            return total + mature(a) * saved_v[t, a].astype(F32)

        load_saved[t].wait()
        total = repeat(0, AGES, 8, add, jnp.zeros((ROWS, 2 * LANES), F32))
        for h in range(2):
            spawn[t, h] = total[:, halves(h)]
        for copy in spawn_copies(t)[0]:
            copy.start()

    def spawn_turn(t):
        one, two = spawn_copies(t)
        for h in range(2):
            one[h].wait_recv()
            spawn_s[t, h] = spawn[t, h] + spawn_a[t, h]
            two[h].start()

    aged.wait()
    spawn_part(1)

    body = slice(0, ROWS)
    for copy in fetches[:3]:
        copy.wait()
    for h in range(2):
        sea[h] = sea_in[:, halves(h)].astype(F32)
    last_lane = lane_all == LANES - 1
    sea0, sea1 = sea[0], sea[1]
    turned1 = pltpu.roll(sea1, LANES - 1, 1)
    open_e[0] = sea0 * jnp.where(last_lane, turned1, pltpu.roll(sea0, LANES - 1, 1))
    open_e[1] = sea1 * jnp.where(last_lane, 0.0, turned1)
    last_row = iota((ROWS, LANES), 0) == ROWS - 1
    pad = jnp.zeros((PAD, LANES), F32)
    for h, here in enumerate((sea0, sea1)):
        open_s[h] = here * jnp.where(last_row, 0.0, pltpu.roll(here, ROWS - 1, 0))
        flow[0, h, 0:PAD, :] = pad
        flow[1, h, 0:PAD, :] = pad
        for t in range(2):
            forage[t, h] = here * prey[t, :, halves(h)]
            warm[t, h] = heat[t, :, halves(h)] * 0.25

    def field(f, h):
        if f == 4:
            return sea[h]
        return (forage, warm)[f % 2][1 - f // 2, h]

    columns = jnp.zeros((ROWS, LANES), F32)
    for h in range(2):
        row_n1[h, 0:8, :] = pad
        row_s1[h, 0:8, :] = pad
    for f in range(5):
        for h in range(2):
            plane = field(f, h)
            row_n1[h, f:f + 1, :] = plane[0:1]
            row_s1[h, f:f + 1, :] = plane[ROWS - 1:ROWS]
        columns = jnp.where(lane_all == FIELD_LANE + 2 * f, jnp.broadcast_to(field(f, 0)[:, 0:1], (ROWS, LANES)), columns)
        columns = jnp.where(
            lane_all == FIELD_LANE + 2 * f + 1, jnp.broadcast_to(field(f, 1)[:, LANES - 1:], (ROWS, LANES)), columns
        )

    def clear_pads(ref, a):
        for h in range(2):
            ref[a, h, ROWS:, :] = pad

    def pick_columns(a, x0, x1):
        width = iota(x0.shape, 1)
        edges = jnp.where(width == 0, x0, x1)
        return ((width + 1) & 127) >> 1 == a, pltpu.roll(edges, 2 * a, 1)

    def eastward(x0, x1):
        turned1 = pltpu.roll(x1, LANES - 1, 1)
        edge = iota(x0.shape, 1) == LANES - 1
        return jnp.where(edge, turned1, pltpu.roll(x0, LANES - 1, 1)), turned1

    load_final.wait()

    def unpack(a, columns):
        x = final_v[a].astype(F32)
        x0, x1 = x[:, :LANES], x[:, LANES:]
        clear_pads(adj1, a)
        clear_pads(adj0, a)
        for h, xh in enumerate((x0, x1)):
            adj1[a, h, body, :] = xh
            row_n1[h, pl.ds(FIRST_AGE + a, 1), :] = xh[0:1]
            row_s1[h, pl.ds(FIRST_AGE + a, 1), :] = xh[ROWS - 1:]
        mine, moved = pick_columns(a, x0, x1)
        return jnp.where(mine, moved, columns)

    col1[...] = repeat(0, AGES, 8, unpack, columns)
    clear_pads(adj1, AGES)
    clear_pads(adj0, AGES)

    def month_copies(t):
        k = k_month + 12 * (1 - t)
        adj = (adj0, adj1)[t]
        col = (col0, col1)[t]
        span = slice(0, 40) if t == 1 else slice(FIRST_AGE, 40)
        row_n, row_s = ((row_n0, row_s0), (row_n1, row_s1))[t]
        halo_n, halo_s = ((halo_n0, halo_s0), (halo_n1, halo_s1))[t]
        diag_n, diag_s = ((diag_n0, diag_s0), (diag_n1, diag_s1))[t]
        col_w, col_e = ((col_w0, col_e0), (col_w1, col_e1))[t]
        dcol_w, dcol_e = ((dcol_w0, dcol_e0), (dcol_w1, dcol_e1))[t]
        first = (first0, first1)[t]
        side = [
            remote(row_n.at[:, span, :], halo_s.at[:, span, :], k, at(c, i_dn, j)),
            remote(row_s.at[:, span, :], halo_n.at[:, span, :], k + 1, at(c, i_up, j)),
            remote(col, col_e, k + 4, at(c, i, j_dn)),
            remote(col, col_w, k + 5, at(c, i, j_up)),
        ]
        younger = [
            remote(adj.at[0, :, body, :], adj.at[AGES, :, body, :], k + 8, at(c_dn, i, j)),
            remote(adj.at[0, :, 0:8, :], diag_s, k + 2, at(c_dn, i_dn, j)),
            remote(adj.at[0, :, ROWS - 8:ROWS, :], diag_n, k + 3, at(c_dn, i_up, j)),
            remote(col, dcol_e, k + 6, at(c_dn, i, j_dn)),
            remote(col, dcol_w, k + 7, at(c_dn, i, j_up)),
        ]
        root = [remote(adj.at[0, :, body, :], first, k + 8 + d, at(d, i, j)) for d in range(1, n_coh)]
        return side, younger, root

    def start_planes(t):
        side, younger, root = month_copies(t)
        adj, first = (adj0, adj1)[t], (first0, first1)[t]

        @pl.when(c > 0)
        def _():
            for copy in younger[:3]:
                copy.start()

        @pl.when(c == 0)
        def _():
            for copy in root:
                copy.start()
            for h in range(2):
                first[h] = adj[0, h, body, :]

    def start_edges(t):
        side, younger, root = month_copies(t)
        for copy in side:
            copy.start()

        @pl.when(c > 0)
        def _():
            for copy in younger[3:]:
                copy.start()

    start_planes(1)
    start_edges(1)

    for copy in others:
        copy.wait()
    spawn_part(0)
    fish_out[...] = fish[...]
    seniority = (c * AGES + iota((AGES, LANES), 0) + 1).astype(F32) * (1.0 / total_ages)
    consts[0] = jnp.broadcast_to(as_column(death_v[...]) * -LOG2E, (AGES, LANES))
    consts[1] = jnp.broadcast_to(as_column(gear_v[...]) * LOG2E, (AGES, LANES))
    consts[2] = jnp.broadcast_to(as_column(breed_v[...]), (AGES, LANES)) * seniority

    def habitats(t):
        def step(a, carry):
            drift_a, level_a = drift[a], level[a] * 0.25
            for r in range(0, ROWS, BY):
                rows = slice(r, r + BY)
                found = []
                for h in range(2):
                    q = warm[t, h, rows, :] - level_a
                    found.append(forage[t, h, rows, :] * drift_a / (1.0 + q * q))
                    hab[a, h, rows, :] = found[h]
                if t == 0:
                    for h, ahead in enumerate(eastward(*found)):
                        hab_e[a, h, rows, :] = ahead
            if t == 1:
                clear_pads(hab, a)
            return carry

        repeat(0, AGES, 4, step, 0)

    def interior(t, adj, into, a, flow):
        spread_a = spread[a]
        for r in range(0, ROWS, BY):
            mid, dn = slice(r, r + BY), slice(r + 1, r + 1 + BY)
            h0, h1 = hab[a, 0, mid, :], hab[a, 1, mid, :]
            l0, l1 = adj[a + 1, 0, mid, :], adj[a + 1, 1, mid, :]
            lr0, lr1 = eastward(l0, l1)
            hr0, hr1 = eastward(h0, h1) if t == 1 else (hab_e[a, 0, mid, :], hab_e[a, 1, mid, :])
            kept, given = [], []
            for h, hh, ll, hr, lr in ((0, h0, l0, hr0, lr0), (1, h1, l1, hr1, lr1)):
                g = hr - hh
                k = jnp.maximum(g, 0.0) + spread_a
                o = open_e[h, mid, :] * (ll - lr)
                y = ll - k * o
                given.append((k - g) * o)
                g = hab[a, h, dn, :] - hh
                k = jnp.maximum(g, 0.0) + spread_a
                o = open_s[h, mid, :] * (ll - adj[a + 1, h, dn, :])
                flow[h, dn, :] = (k - g) * o
                kept.append(y - k * o)
            m0, m1 = pltpu.roll(given[0], 1, 1), pltpu.roll(given[1], 1, 1)
            into[a, 0, mid, :] = kept[0] + (flow[0, mid, :] + jnp.where(lane == 0, m1, m0))
            into[a, 1, mid, :] = kept[1] + (flow[1, mid, :] + jnp.where(lane == 0, m0, m1))

    def interiors(t, lo, hi):
        adj, into = (adj0, adj1)[t], (rest, rest1)[t]
        turns = itertools.count()

        def step(a, carry):
            interior(t, adj, into, a, flow.at[next(turns) % 2])
            return carry

        repeat(lo, hi, 2, step, 0)

    age_of = iota((AGES, LANES), 0)
    lane_age = ((iota((AGES, LANES), 1) + 1) & 127) >> 1

    def by_row(v):
        return as_column(v[...])

    def by_lane(v):
        wide = jnp.broadcast_to(by_row(v), (AGES, LANES))
        return jnp.sum(jnp.where(age_of == lane_age, wide, 0.0), axis=0, keepdims=True)

    north_open = jnp.where(i > 0, 1.0, 0.0)
    south_open = jnp.where(i < n_lat - 1, 1.0, 0.0)
    west_open = jnp.where(j > 0, 1.0, 0.0)
    east_open = jnp.where(j < n_lon - 1, 1.0, 0.0)

    def edges(t):
        adj = (adj0, adj1)[t]
        side, younger, root = month_copies(t)
        halo_n, halo_s = ((halo_n0, halo_s0), (halo_n1, halo_s1))[t]
        row_n, row_s = ((row_n0, row_s0), (row_n1, row_s1))[t]
        diag_n, diag_s = ((diag_n0, diag_s0), (diag_n1, diag_s1))[t]
        col = (col0, col1)[t]
        col_w, col_e = ((col_w0, col_e0), (col_w1, col_e1))[t]
        dcol_w, dcol_e = ((dcol_w0, dcol_e0), (dcol_w1, dcol_e1))[t]
        for copy in side:
            copy.wait_recv()

        @pl.when(c < n_coh - 1)
        def _():
            for copy in younger[1:]:
                copy.wait_recv()

        @pl.when(c == n_coh - 1)
        def _():
            diag_n[...] = jnp.zeros_like(diag_n)
            diag_s[...] = jnp.zeros_like(diag_s)
            dcol_w[...] = jnp.zeros_like(dcol_w)
            dcol_e[...] = jnp.zeros_like(dcol_e)

        past = FIRST_AGE + AGES
        for h in range(2):
            row_n[h, past:past + 1, :] = adj[AGES, h, 0:1, :]
            row_s[h, past:past + 1, :] = adj[AGES, h, ROWS - 1:ROWS, :]
            halo_n[h, past:past + 1, :] = diag_n[h, 7:8, :]
            halo_s[h, past:past + 1, :] = diag_s[h, 0:1, :]
        later = slice(FIRST_AGE + 1, FIRST_AGE + 1 + AGES)
        f = 2 * (1 - t)
        to_col, to_n, to_s = ((fix_col, fix_n, fix_s), (fix_col1, fix_n1, fix_s1))[t]
        spread_r, drift_r, level_r = (
            jnp.broadcast_to(x, (AGES, LANES)) for x in (by_row(spread_v), by_row(drift_v), by_row(level_v) * 0.25)
        )
        for own, halo, own1, halo1, gate, fix in (
            (row_n, halo_n, row_n1, halo_n1, north_open, to_n),
            (row_s, halo_s, row_s1, halo_s1, south_open, to_s),
        ):
            for h in range(2):
                def habitat(buf):
                    q = buf[h, f + 1:f + 2, :] - level_r
                    return buf[h, f:f + 1, :] * drift_r / (1.0 + q * q)

                passage = own1[h, 4:5, :] * halo1[h, 4:5, :] * gate
                k = spread_r + jnp.maximum(habitat(halo1) - habitat(own1), 0.0)
                fix[h] = passage * k * (own[h, later, :] - halo[h, later, :])

        def both(own_w, own_e):
            wide = (ROWS, LANES)
            return jnp.where(even_all, jnp.broadcast_to(own_w, wide), jnp.broadcast_to(own_e, wide))

        def own_field(f):
            return both(field(f, 0)[:, 0:1], field(f, 1)[:, LANES - 1:])

        def halo_field(f):
            spot = FIELD_LANE + 2 * f
            return both(col_w1[:, spot + 1:spot + 2], col_e1[:, spot:spot + 1])

        spread_l, drift_l, level_l = (by_lane(x) for x in (spread_v, drift_v, level_v))

        def habitat_columns(get):
            q = get(f + 1) - level_l * 0.25
            return get(f) * drift_l / (1.0 + q * q)

        passage = own_field(4) * halo_field(4) * jnp.where(even_all, west_open, east_open)
        mine, moved = pick_columns(AGES, adj[AGES, 0, body, :], adj[AGES, 1, body, :])
        own = pltpu.roll(jnp.where(mine, moved, col[...]), LANES - 2, 1)
        other = jnp.where(even_all, pltpu.roll(col_w[...], LANES - 1, 1), pltpu.roll(col_e[...], LANES - 3, 1))
        other = jnp.where(lane_all == 62, pltpu.roll(dcol_w[...], 63, 1), other)
        other = jnp.where(lane_all == 61, pltpu.roll(dcol_e[...], 61, 1), other)
        k = spread_l + jnp.maximum(habitat_columns(halo_field) - habitat_columns(own_field), 0.0)
        fix = passage * k * (own - other)
        for a in range(AGES):
            to_col[a] = pltpu.roll(fix, (LANES - 2 * a) % LANES, 1)

    def finish_one():
        def put(b, a, columns, recruits, catches):
            made = finished(b, a, rest1, fix_col1, fix_n1, fix_s1, blocks1, 0, recruits, catches, consts)
            for h in range(2):
                adj0[a, h, b * BY:(b + 1) * BY, :] = made[h]
                if b == 0:
                    row_n0[h, pl.ds(FIRST_AGE + a, 1), :] = made[h][0:1]
                if b == ROWS // BY - 1:
                    row_s0[h, pl.ds(FIRST_AGE + a, 1), :] = made[h][BY - 1:]
            mine, moved = pick_columns(a, made[0], made[1])
            return jnp.where(mine, moved, columns)

        def block(b):
            rows = slice(b * BY, (b + 1) * BY)
            return rows, [rec1[h, rows, :] for h in range(2)], [fish[rows, halves(h)] for h in range(2)]

        for b in range(ROWS // BY):
            rows, recruits, catches = block(b)
            col0[rows, :] = put(b, 0, jnp.zeros((BY, LANES), F32), recruits, catches)
        start_planes(0)
        for b in range(ROWS // BY):
            rows, recruits, catches = block(b)

            def step(group, columns):
                for n in range(GROUP):
                    columns = put(b, group * GROUP + n, columns, recruits, catches)
                return columns

            columns = col0[rows, :]
            for a in range(1, GROUP):
                columns = put(b, a, columns, recruits, catches)
            col0[rows, :] = lax.fori_loop(1, AGES // GROUP, step, columns)
        start_edges(0)

    def last_cohort(t):
        adj = (adj0, adj1)[t]
        side, younger, root = month_copies(t)

        @pl.when(c < n_coh - 1)
        def _():
            younger[0].wait_recv()

        @pl.when(c == n_coh - 1)
        def _():
            for h in range(2):
                adj[AGES, h, body, :] = jnp.zeros((ROWS, LANES), F32)

        interiors(t, AGES - 1, AGES)

    def recruit(t):
        first = (first0, first1)[t]
        side, younger, root = month_copies(t)
        for d in range(1, n_coh):
            @pl.when(c == d)
            def _():
                root[d - 1].wait_recv()
        two = spawn_copies(t)[1]
        for h in range(2):
            two[h].wait_recv()
            total = spawn_s[t, h] + spawn_b[t, h]
            ratio = 1.0 / (1.0 + total)
            base = first[h] * sea[h]
            (rec, rec1)[t][h] = base * offspring[:, halves(h)] * ratio * ratio
            gain = base * total * ratio
            if t == 1:
                grad[:, halves(h)] = gain
            else:
                grad[:, halves(h)] = grad[:, halves(h)] + gain

    fold_sends = [
        remote(fold_out.at[lax.rem(i + d, n_lat)], fold_in.at[i], k_fold + d, at(c, lax.rem(i + d, n_lat), j))
        for d in range(1, n_lat)
    ]

    habitats(1)
    spawn_turn(1)
    interiors(1, 0, 10)
    for copy in catch_sends:
        copy.wait_recv()
    got = catch_in[...].reshape(slots, LANES)
    half = n_lat * 16
    code_row = as_row(got[:, CODE:CODE + 1])
    wanted = iota((2 * half, slots), 0)
    low = wanted & (half - 1)
    code = ((low >> 4) * 32 + (low & 15) + jnp.where(wanted < half, 0, 16)).astype(F32)
    pick = jnp.where(code == jnp.broadcast_to(code_row, (2 * half, slots)), 1.0, 0.0)
    folded = selected(pick, got)
    packed = jnp.where(iota((half, LANES), 1) < 64, folded[:half], pltpu.roll(folded[half:], 64, 1))
    fold_out[...] = packed.reshape(n_lat, 16, LANES)
    fold_in[i] = fold_out[i]
    for copy in fold_sends:
        copy.start()
    interiors(1, 10, AGES - 1)
    last_cohort(1)
    habitats(0)
    edges(1)
    spawn_turn(0)
    recruit(1)
    for copy in fold_sends:
        copy.wait_recv()
    block = fold_in[0]
    for d in range(1, n_lat):
        block = block + fold_in[d]
    block = jnp.concatenate([block, pltpu.roll(block, 64, 1)], axis=0)
    cells = 2 * LANES * (ROWS // BY)

    def spread_blocks(t, to):
        stack = jnp.concatenate(
            [part.astype(F32) for part in parts(block[:, t * AGES:(t + 1) * AGES])], axis=0
        ).astype(jnp.bfloat16)
        widen = jnp.where((iota((96, cells), 0) & 31) == iota((96, cells), 1) >> 5, 1.0, 0.0).astype(jnp.bfloat16)
        planes = lax.dot_general(stack, widen, (((0,), (0,)), ((), ())), preferred_element_type=F32)
        gear_r = jnp.broadcast_to(by_row(gear_v), (AGES, LANES))
        for b in range(cells // LANES):
            to[b] = planes[:, b * LANES:(b + 1) * LANES] * gear_r

    spread_blocks(1, blocks1)
    finish_one()

    interiors(0, 0, AGES - 1)
    spread_blocks(0, blocks)
    last_cohort(0)
    edges(0)
    recruit(0)

    for copy in catch_sends + fold_sends:
        copy.wait_send()
    for t in range(2):
        side, younger, root = month_copies(t)
        one, two = spawn_copies(t)
        for copy in side + one + two:
            copy.wait_send()

        @pl.when(c > 0)
        def _():
            for copy in younger:
                copy.wait_send()

        @pl.when(c == 0)
        def _():
            for copy in root:
                copy.wait_send()

def combine(rest, fix_col, fix_n, fix_s, rec, blocks, consts, fish, grad, out, grad_out, out_v, out_sem):
    ends = [pltpu.make_async_copy(grad, grad_out, out_sem.at[ROWS // BY])]
    ends[0].start()
    for b in range(ROWS // BY):
        rows = slice(b * BY, (b + 1) * BY)
        recruits = [rec[h, rows, :] for h in range(2)]
        catches = [fish[rows, halves(h)] for h in range(2)]

        def step(a, carry):
            made = finished(b, a, rest, fix_col, fix_n, fix_s, blocks, 0, recruits, catches, consts)
            for h in range(2):
                out_v[a, rows, halves(h)] = made[h]
            return carry

        repeat(0, AGES, GROUP, step, 0)
        span = pl.ds(b * BY, BY)
        ends.append(pltpu.make_async_copy(out_v.at[:, span, :], out.at[:, span, :], out_sem.at[b]))
        ends[-1].start()
    for copy in ends:
        copy.wait()


def shards(
    sizes,
    saved, final, prey, heat, sea, fish, offspring,
    death, gear, spread, drift, level, breed,
    landing, east, north, patch, bounds,
):
    n_coh, n_lat, n_lon = sizes
    hbm = pl.BlockSpec(memory_space=pltpu.HBM)
    vmem = pl.BlockSpec(memory_space=pltpu.VMEM)
    given = [
        prey, heat, sea, fish, offspring, spread, drift, level, breed,
        *[v.reshape(1, -1) for v in (gear, spread, drift, level, death, breed)],
        landing, *[v.reshape(1, -1) for v in (east, north, patch)], bounds.T,
    ]
    spaces = [pltpu.VMEM] * 5 + [pltpu.SMEM] * 4 + [pltpu.VMEM] * 11
    plane = (2, ROWS, LANES)
    padded = (AGES + 1, 2, ROWS + PAD, LANES)
    edge_rows, tile, column = (2, 48, LANES), (2, 8, LANES), (ROWS, LANES)
    made = [
        (AGES, *plane), (AGES, *column), (2, AGES, LANES), (2, AGES, LANES), plane,
        (2 * ROWS // BY, AGES, LANES), (3, AGES, LANES), (ROWS, 2 * LANES), (ROWS, 2 * LANES),
    ]

    def f32(shape):
        return pltpu.VMEM(shape, F32)

    scratch = [space(v.shape, v.dtype) for space, v in zip(spaces, given)] + [
        pltpu.VMEM((2, AGES, ROWS, 2 * LANES), jnp.bfloat16),
        pltpu.VMEM((AGES, ROWS, 2 * LANES), jnp.bfloat16),
        f32(padded), f32(padded), f32(made[0]), f32(padded), f32(made[0]), f32((2, 2, ROWS + PAD, LANES)),
        f32((2, *plane)), f32((2, *plane)), f32(plane), f32(plane), f32(plane), f32(plane),
        *[f32(edge_rows) for _ in range(8)],
        *[f32(tile) for _ in range(4)],
        *[f32(column) for _ in range(10)],
        f32(made[1]), f32(made[2]), f32(made[3]),
        f32(plane), f32(plane), *[f32((2, *plane)) for _ in range(4)],
        f32((32, LANES)), f32((n_lon, SLOTS, LANES)), f32((n_lon, SLOTS, LANES)),
        f32((n_lat, 16, LANES)), f32((n_lat, 16, LANES)),
        f32(made[5]),
        pltpu.SemaphoreType.DMA((3 + GIVEN,)),
        pltpu.SemaphoreType.DMA((52,)),
        pltpu.SemaphoreType.DMA((52,)),
    ]
    states = pl.pallas_call(
        functools.partial(kernel, sizes),
        out_shape=[jax.ShapeDtypeStruct(shape, F32) for shape in made],
        in_specs=[hbm] * (2 + GIVEN),
        out_specs=[vmem] * len(made),
        scratch_shapes=scratch,
        compiler_params=pltpu.CompilerParams(
            collective_id=0, has_side_effects=True, vmem_limit_bytes=32 * 1024 * 1024
        ),
    )(*[pltpu.with_memory_space_constraint(v, pltpu.HBM) for v in (saved, final, *given)])
    return pl.pallas_call(
        combine,
        out_shape=(
            jax.ShapeDtypeStruct((AGES, ROWS, 2 * LANES), F32),
            jax.ShapeDtypeStruct((ROWS, 2 * LANES), F32),
        ),
        in_specs=[vmem] * len(made),
        out_specs=(hbm, hbm),
        scratch_shapes=[f32((AGES, ROWS, 2 * LANES)), pltpu.SemaphoreType.DMA((ROWS // BY + 1,))],
        compiler_params=pltpu.CompilerParams(vmem_limit_bytes=8 * 1024 * 1024),
    )(*states)


def solution(mesh):
    sizes = tuple(mesh.shape[axis] for axis in ("coh", "lat", "lon"))
    tile = P("lat", "lon")
    months = P(None, "lat", "lon")
    rows = ("lat", "lon")
    in_specs = (
        P(None, "coh", "lat", "lon"), P("coh", "lat", "lon"), months, months, tile, tile, tile,
        *[P("coh")] * 6,
        P(rows, None, "coh"), P(rows, None), P(rows), P(rows), P(rows, None),
    )
    out_specs = (P("coh", "lat", "lon"), tile)
    return jax.shard_map(
        functools.partial(shards, sizes), mesh=mesh, in_specs=in_specs, out_specs=out_specs, check_vma=False
    )
```
